32 devices in a mesh: grp: 2 (over x), seq: 16 (over z, y, core).
Axes of the slice: x: 2, y: 2, z: 4, core: 2. Of those that a mesh axis runs over, the one named last changes fastest.
Arguments:
- image_qkv: bfloat16 [3, 8, 16, 896, 128], P(None, 'grp', None, 'seq'), parts along dimension 1, may hold values from -16 to 16
- text_kv: bfloat16 [2, 2, 8, 16, 512, 128], P(None, None, 'grp', None, 'seq'), parts along dimension 2, may hold values from -6 to 6
- prompt_ids: int32 [2, 8, 512], P(None, 'grp'), parts along dimension 1, may hold values from 0 to 32127, as said below
- timesteps: int32 [8], P('grp'), parts along dimension 0, may hold values from 0 to 999
- image_states: bfloat16 [8, 896, 1536], P('grp', 'seq'), parts along dimension 0, may hold values from -6 to 6
- frozen_out: bfloat16 [2048, 1536], P('seq'), may hold values from -0.125 to 0.125
- trainee_out: bfloat16 [4096, 1536], P(('grp', 'seq')), parts along dimension 0, may hold values from -0.125 to 0.125
- time_mod: bfloat16 [256, 3072], replicated, may hold values from -0.375 to 0.375
- final_head: bfloat16 [1536, 64], replicated, may hold values from -0.15625 to 0.15625
Outputs:
- weight_grad: float32 [4096, 1536], P(('grp', 'seq')), parts along dimension 0
The draws below stay inside these ranges and needn't reach their ends.
There are 2 independent parts, one for each index of `grp`. The reference program is written for one: setup_inputs(seed, part) draws one part's arguments, and reference() takes and returns one part's arrays. A program takes and returns all parts, laid end to end along the dimension named above; an argument that names none is the same for every part. Nothing has to cross between parts.
Inputs may be any that keep to these rules, and one draw needn't show every extreme that they name: `prompt_ids`: zero marks padding; in each row of 512 ids the padding is a suffix and position 0 is never padding.
All inputs are finite; a program needn't handle non-finite values.
Results may differ from the reference program's by a relative error of at most 0.011.
Values may be sent and summed in bfloat16 or wider, within the bound.
No kernel may reach another device: no remote copies, remote signals or barrier semaphores. Data moves between devices by JAX's collectives and lax.ppermute only.
A program may use at most 128 MiB of HBM per device.

```python
import math
import jax
import jax.numpy as jnp
from jax import lax

SAMPLES = 4
HEADS = 16
HEAD_DIM = 128
WIDTH = 1536
CHANNELS = 64
TIME_DIM = 256
TEXT = 512
VOCABULARY = 32128
IMAGE = 896
INNER = 2048


def draw_image_qkv(key, part):
    key_base = jax.random.fold_in(key, 0)
    shape = (3, SAMPLES, HEADS, IMAGE, HEAD_DIM)
    result = jnp.clip(jax.random.normal(key_base, shape, jnp.float32), -4.0, 4.0)
    return result.astype(jnp.bfloat16)


def draw_prompt_ids(key, part):
    key_length, key_tokens = jax.random.split(key, 2)
    lengths = jax.random.randint(key_length, (2, SAMPLES, 1), 1, TEXT + 1)
    lengths = lengths.at[1, 0, 0].set(TEXT // 2)
    tokens = jax.random.randint(key_tokens, (2, SAMPLES, TEXT), 1, VOCABULARY)
    tokens = tokens.at[0, 0, 0].set(VOCABULARY - 1)
    position = jnp.arange(TEXT, dtype=jnp.int32)[None, None, :]
    return jnp.where(position < lengths, tokens, 0).astype(jnp.int32)


def place_ends(entries, stream_key, smallest, largest):
    longest = entries.shape.index(max(entries.shape))
    spots = []
    for shift in (0, 1):
        where = [jax.random.randint(jax.random.fold_in(stream_key, axis), (), 0, length) for axis, length in enumerate(entries.shape)]
        where[longest] = (where[longest] + shift) % entries.shape[longest]
        spots.append(tuple(where))
    return entries.at[spots[0]].set(smallest).at[spots[1]].set(largest)


def levels(rng, extent, cuts, least, top_value):
    loudness, own = 1.0, jax.random.fold_in(rng, 6)
    for dim, parts in cuts:
        draws = jnp.exp(jax.random.uniform(jax.random.fold_in(own, dim), (parts,), jnp.float32, least / len(cuts), top_value / len(cuts)))
        loudness = loudness * jnp.repeat(draws, extent[dim] // parts).reshape([-1 if axis == dim else 1 for axis in range(len(extent))])
    return loudness


def normal_values(stream_key, dims, scale, reach, cuts=(), held_as=jnp.bfloat16):
    loudness = levels(stream_key, dims, cuts, -0.22, 0.18) if cuts else 1.0
    entries = jax.random.normal(stream_key, dims, jnp.float32) * scale * loudness
    return jnp.minimum(jnp.maximum(entries, -reach), reach).astype(held_as)


def setup_inputs(seed: int = 0, part: int = 0) -> dict:
    key_list = jax.random.split(jax.random.key(seed), 10)
    part_keys = jax.random.split(jax.random.fold_in(key_list[9], part), 10)
    image_qkv = draw_image_qkv(jax.random.fold_in(jax.random.fold_in(key_list[9], part), 71), part)
    text_kv = normal_values(part_keys[1], (2, 2, SAMPLES, HEADS, TEXT, HEAD_DIM), 1.0, 6.0, ((4, 16),))
    prompt_ids = draw_prompt_ids(jax.random.fold_in(jax.random.fold_in(key_list[9], part), 71), part)
    timesteps = place_ends(jax.random.randint(part_keys[3], (SAMPLES,), 0, 1000), jax.random.fold_in(part_keys[3], 1), 0, 999).astype(jnp.int32)
    image_states = normal_values(part_keys[4], (SAMPLES, IMAGE, WIDTH), 1.0, 6.0, ((1, 16),))
    frozen_out = normal_values(key_list[5], (INNER, WIDTH), INNER ** -0.5, 0.125, ((0, 16),))
    trainee_out = normal_values(part_keys[6], (INNER, WIDTH), INNER ** -0.5, 0.125, ((0, 16),))
    time_mod = normal_values(key_list[7], (TIME_DIM, 2 * WIDTH), TIME_DIM ** -0.5, 0.375)
    final_head = normal_values(key_list[8], (WIDTH, CHANNELS), WIDTH ** -0.5, 0.15625)
    return {"image_qkv": image_qkv, "text_kv": text_kv, "prompt_ids": prompt_ids, "timesteps": timesteps, "image_states": image_states, "frozen_out": frozen_out, "trainee_out": trainee_out, "time_mod": time_mod, "final_head": final_head}


def attend_pair(queries, image_keys, image_values, text_keys, text_values, allowed_text):
    factor = HEAD_DIM ** (-0.5)
    image_scores = jnp.dot(queries, image_keys.T, preferred_element_type=jnp.float32) * factor
    image_max = lax.optimization_barrier(jnp.max(image_scores, axis=1, keepdims=True))
    image_exp = jnp.exp(image_scores - image_max)
    image_total = lax.optimization_barrier(jnp.sum(image_exp, axis=1, keepdims=True))
    image_part = jnp.dot(image_exp.astype(jnp.bfloat16), image_values, preferred_element_type=jnp.float32)
    results = []
    for pass_index in range(2):
        text_scores = jnp.dot(queries, text_keys[pass_index].T, preferred_element_type=jnp.float32) * factor
        text_scores = jnp.where(allowed_text[pass_index][None, :], text_scores, -jnp.inf)
        pass_max = jnp.maximum(image_max, lax.optimization_barrier(jnp.max(text_scores, axis=1, keepdims=True)))
        ratio = jnp.exp(image_max - pass_max)
        text_exp = jnp.exp(text_scores - pass_max)
        text_part = jnp.dot(text_exp.astype(jnp.bfloat16), text_values[pass_index], preferred_element_type=jnp.float32)
        numer = ratio * image_part + text_part
        denom = ratio * image_total + lax.optimization_barrier(jnp.sum(text_exp, axis=1, keepdims=True))
        results.append((numer / denom).astype(jnp.bfloat16))
    return jnp.stack(results)

def head_out(branch, states, gate, scale, final_head):
    mixed = states.astype(jnp.float32) + gate[:, None, :] * branch
    normed = mixed * lax.rsqrt(lax.optimization_barrier(jnp.mean(mixed * mixed, axis=-1, keepdims=True)) + 1e-06) * (1.0 + scale[:, None, :])
    normed = normed.astype(jnp.bfloat16)
    return jnp.einsum('bic,cd->bid', normed.astype(jnp.float32), final_head.astype(jnp.float32))

def reference(image_qkv, text_kv, prompt_ids, timesteps, image_states, frozen_out, trainee_out, time_mod, final_head):
    live = prompt_ids != 0

    def per_item(item_index):
        sample = item_index // HEADS
        head_index = item_index % HEADS
        text_keys = jnp.stack([text_kv[0, 0, sample, head_index], text_kv[1, 0, sample, head_index]])
        text_values = jnp.stack([text_kv[0, 1, sample, head_index], text_kv[1, 1, sample, head_index]])
        allowed = jnp.stack([live[0, sample], live[1, sample]])
        return attend_pair(image_qkv[0, sample, head_index], image_qkv[1, sample, head_index], image_qkv[2, sample, head_index], text_keys, text_values, allowed)
    attention = lax.map(per_item, jnp.arange(SAMPLES * HEADS, dtype=jnp.int32))
    attention = attention.reshape(SAMPLES, HEADS, 2, IMAGE, HEAD_DIM).transpose(2, 0, 3, 1, 4)
    attention = attention.reshape(2, SAMPLES * IMAGE, INNER)
    half_dim = TIME_DIM // 2
    freqs = jnp.exp(-math.log(10000.0) * jnp.arange(half_dim, dtype=jnp.float32) / half_dim)
    angles = timesteps.astype(jnp.float32)[:, None] * freqs[None, :]
    embedding = jnp.concatenate([jnp.cos(angles), jnp.sin(angles)], 1)
    modulation = jnp.dot(embedding, time_mod.astype(jnp.float32), precision=lax.Precision.HIGHEST)
    gate = modulation[:, :WIDTH]
    scale = modulation[:, WIDTH:]
    branch_c = jnp.dot(attention[0], frozen_out, preferred_element_type=jnp.float32).reshape(SAMPLES, IMAGE, WIDTH)
    branch_n = jnp.dot(attention[1], frozen_out, preferred_element_type=jnp.float32).reshape(SAMPLES, IMAGE, WIDTH)
    branch_s = jnp.dot(attention[0], trainee_out, preferred_element_type=jnp.float32).reshape(SAMPLES, IMAGE, WIDTH)
    velocity_c = head_out(branch_c, image_states, gate, scale, final_head)
    velocity_n = head_out(branch_n, image_states, gate, scale, final_head)
    target = velocity_n - (velocity_c - velocity_n)

    def student(branch):
        velocity_s = head_out(branch, image_states, gate, scale, final_head)
        return jnp.sum((velocity_s - target) ** 2) / SAMPLES
    loss, pull = jax.vjp(student, branch_s)
    cotangent, = pull(jnp.ones_like(loss))
    cotangent = cotangent.reshape(SAMPLES * IMAGE, WIDTH).astype(jnp.bfloat16)
    return jnp.dot(attention[0].T, cotangent, preferred_element_type=jnp.float32)
```

```python
import functools
import math

import jax
import jax.numpy as jnp
from jax import lax
from jax.experimental import pallas as pl
from jax.experimental.pallas import tpu as pltpu
from jax.sharding import PartitionSpec as P

SAMPLES = 4
HEADS = 16
HEAD_DIM = 128
WIDTH = 1536
TIME_DIM = 256
LOG2E = math.log2(math.e)


def attention_kernel(image_dev, text_dev, block_rows, x_ref, live_ref, out_ref, q_s, k_s, v_s, tk_s, tv_s):
    sources = x_ref.shape[0]
    image_all = sources * image_dev
    text_all = sources * text_dev
    block = pl.program_id(1)

    @pl.when(block == 0)
    def _():
        def rows(start, count):
            piece = x_ref[:, 0, start:start + count, :].astype(jnp.float32)
            return piece.reshape(sources * count, HEAD_DIM).astype(jnp.bfloat16)

        ones_image = jnp.ones((image_all, HEAD_DIM), jnp.bfloat16)
        ones_text = jnp.ones((text_all, HEAD_DIM), jnp.bfloat16)
        for p in range(2):
            tk_s[p] = rows(2 * p * text_dev, text_dev)
            tv_s[p, :, :HEAD_DIM] = rows((2 * p + 1) * text_dev, text_dev)
            tv_s[p, :, HEAD_DIM:] = ones_text
        base = 4 * text_dev
        q_s[...] = rows(base, image_dev)
        k_s[...] = rows(base + image_dev, image_dev)
        v_s[:, :HEAD_DIM] = rows(base + 2 * image_dev, image_dev)
        v_s[:, HEAD_DIM:] = ones_image

    factor = HEAD_DIM ** (-0.5) * LOG2E
    contract = (((1,), (1,)), ((), ()))
    start = pl.multiple_of(block * block_rows, 16)
    queries = q_s[pl.ds(start, block_rows), :]
    scores = lax.dot_general(queries, k_s[...], contract, preferred_element_type=jnp.float32)
    image_max = jnp.max(scores, axis=1, keepdims=True) * factor
    weights = jnp.exp2(scores * factor - image_max).astype(jnp.bfloat16)
    image_out = jnp.dot(weights, v_s[...], preferred_element_type=jnp.float32)
    for p in range(2):
        text = lax.dot_general(queries, tk_s[p], contract, preferred_element_type=jnp.float32)
        text = jnp.where(live_ref[0, p:p + 1, :] != 0, text * factor, -jnp.inf)
        pass_max = jnp.maximum(image_max, jnp.max(text, axis=1, keepdims=True))
        ratio = jnp.exp2(image_max - pass_max)
        text_weights = jnp.exp2(text - pass_max).astype(jnp.bfloat16)
        both = ratio * image_out + jnp.dot(text_weights, tv_s[p], preferred_element_type=jnp.float32)
        result = both[:, :HEAD_DIM] / both[:, HEAD_DIM:]
        out_ref[:, 0, p] = result.reshape(block_rows // image_dev, image_dev, HEAD_DIM).astype(out_ref.dtype)


def attend(gathered, live, image_dev, text_dev):
    sources, owned = gathered.shape[:2]
    rows = gathered.shape[2]
    image_all, text_all = sources * image_dev, sources * text_dev
    per_block = 4
    blocks = sources // per_block
    block_rows = per_block * image_dev
    scores_flops = 2 * image_all * (image_all + 2 * text_all) * HEAD_DIM
    return pl.pallas_call(
        functools.partial(attention_kernel, image_dev, text_dev, block_rows),
        grid=(owned, blocks),
        in_specs=[
            pl.BlockSpec((sources, 1, rows, HEAD_DIM), lambda j, i: (0, j, 0, 0)),
            pl.BlockSpec((1, 2, text_all), lambda j, i: (j, 0, 0)),
        ],
        out_specs=pl.BlockSpec((per_block, 1, 2, image_dev, HEAD_DIM), lambda j, i: (i, j, 0, 0, 0)),
        out_shape=jax.ShapeDtypeStruct((sources, owned, 2, image_dev, HEAD_DIM), jnp.bfloat16),
        scratch_shapes=[
            pltpu.VMEM((image_all, HEAD_DIM), jnp.bfloat16),
            pltpu.VMEM((image_all, HEAD_DIM), jnp.bfloat16),
            pltpu.VMEM((image_all, 2 * HEAD_DIM), jnp.bfloat16),
            pltpu.VMEM((2, text_all, HEAD_DIM), jnp.bfloat16),
            pltpu.VMEM((2, text_all, 2 * HEAD_DIM), jnp.bfloat16),
        ],
        compiler_params=pltpu.CompilerParams(
            dimension_semantics=("arbitrary", "arbitrary"), vmem_limit_bytes=48 << 20
        ),
        cost_estimate=pl.CostEstimate(
            flops=2 * owned * scores_flops,
            bytes_accessed=2 * gathered.size + 4 * owned * image_all * HEAD_DIM,
            transcendentals=owned * image_all * (image_all + 2 * text_all),
        ),
        name="attention",
    )(gathered, live)


def head_out(branch, states, gate, scale, final_head):
    mixed = states.astype(jnp.float32) + gate[:, None, :] * branch
    normed = (
        mixed
        * lax.rsqrt(jnp.mean(mixed * mixed, axis=-1, keepdims=True) + 1e-06)
        * (1.0 + scale[:, None, :])
    )
    normed = normed.astype(jnp.bfloat16)
    return jnp.einsum("bic,cd->bid", normed, final_head, preferred_element_type=jnp.float32)


def shards(
    image_qkv,
    text_kv,
    prompt_ids,
    timesteps,
    image_states,
    frozen_out,
    trainee_out,
    time_mod,
    final_head,
):
    group_size = lax.axis_size("seq")
    position = lax.axis_index("seq")
    image_dev = image_qkv.shape[3]
    text_dev = text_kv.shape[4]
    owned = SAMPLES * HEADS // group_size
    token_rows = SAMPLES * image_dev
    image_items = image_qkv.transpose(2, 1, 0, 3, 4).reshape(group_size, owned, 3 * image_dev, HEAD_DIM)
    text_items = text_kv.transpose(3, 2, 0, 1, 4, 5).reshape(group_size, owned, 4 * text_dev, HEAD_DIM)
    packed = jnp.concatenate([text_items, image_items], axis=2)
    gathered = lax.all_to_all(packed, "seq", split_axis=0, concat_axis=0, tiled=True)
    sample_of = (position * owned + jnp.arange(owned, dtype=jnp.int32)) % SAMPLES
    live = jnp.take(prompt_ids, sample_of, axis=1).transpose(1, 0, 2)
    live = (live != 0).astype(jnp.int32)
    both = attend(gathered, live, image_dev, text_dev)
    returned = lax.all_to_all(both, "seq", split_axis=0, concat_axis=0, tiled=True)
    attention = returned.reshape(HEADS, SAMPLES, 2, image_dev, HEAD_DIM).transpose(2, 1, 3, 0, 4)
    attention = attention.reshape(2, token_rows, HEADS * HEAD_DIM)
    half_dim = TIME_DIM // 2
    freqs = jnp.exp(-math.log(10000.0) * jnp.arange(half_dim, dtype=jnp.float32) / half_dim)
    angles = timesteps.astype(jnp.float32)[:, None] * freqs[None, :]
    embedding = jnp.concatenate([jnp.cos(angles), jnp.sin(angles)], 1)
    modulation = jnp.dot(embedding, time_mod.astype(jnp.float32), precision=lax.Precision.HIGHEST)
    gate = modulation[:, :WIDTH]
    scale = modulation[:, WIDTH:]
    piece_frozen = lax.all_gather(frozen_out, "seq", axis=0, tiled=True)
    piece_trainee = lax.all_gather(trainee_out, "seq", axis=0, tiled=True)
    columns_c = attention[0]
    columns_n = attention[1]
    branch_c = jnp.dot(columns_c, piece_frozen, preferred_element_type=jnp.float32)
    branch_n = jnp.dot(columns_n, piece_frozen, preferred_element_type=jnp.float32)
    branch_s = jnp.dot(columns_c, piece_trainee, preferred_element_type=jnp.float32)
    branch_c = branch_c.reshape(SAMPLES, image_dev, WIDTH)
    branch_n = branch_n.reshape(SAMPLES, image_dev, WIDTH)
    branch_s = branch_s.reshape(SAMPLES, image_dev, WIDTH)
    velocity_c = head_out(branch_c, image_states, gate, scale, final_head)
    velocity_n = head_out(branch_n, image_states, gate, scale, final_head)
    target = velocity_n - (velocity_c - velocity_n)

    def student(branch):
        velocity_s = head_out(branch, image_states, gate, scale, final_head)
        return jnp.sum((velocity_s - target) ** 2) / SAMPLES

    loss_part, pull = jax.vjp(student, branch_s)
    (cotangent,) = pull(jnp.ones_like(loss_part))
    cotangent_rows = cotangent.astype(jnp.bfloat16).reshape(token_rows, WIDTH)
    partial = lax.dot_general(
        columns_c, cotangent_rows, (((0,), (0,)), ((), ())), preferred_element_type=jnp.float32
    ).astype(jnp.bfloat16)
    total = lax.psum_scatter(partial, "seq", scatter_dimension=0, tiled=True)
    return total.astype(jnp.float32)


def solution(mesh):
    return jax.shard_map(
        shards,
        mesh=mesh,
        in_specs=(
            P(None, "grp", None, "seq", None),
            P(None, None, "grp", None, "seq", None),
            P(None, "grp", None),
            P("grp"),
            P("grp", "seq", None),
            P("seq", None),
            P(("grp", "seq"), None),
            P(),
            P(),
        ),
        out_specs=P(("grp", "seq"), None),
        check_vma=False,
    )
```

```python
import functools
import math

import jax
import jax.numpy as jnp
from jax import lax
from jax.experimental import pallas as pl
from jax.experimental.pallas import tpu as pltpu
from jax.sharding import PartitionSpec as P

SAMPLES = 4
HEADS = 16
HEAD_DIM = 128
WIDTH = 1536
TIME_DIM = 256
CHUNKS = 2
LOG2E = math.log2(math.e)


def attention_kernel(image_dev, text_dev, block_rows, x_ref, live_ref, out_ref, q_s, k_s, v_s, tk_s, tv_s):
    sources = x_ref.shape[0]
    image_all = sources * image_dev
    text_all = sources * text_dev
    block = pl.program_id(1)

    @pl.when(block == 0)
    def _():
        def rows(start, count):
            piece = x_ref[:, 0, start:start + count, :].astype(jnp.float32)
            return piece.reshape(sources * count, HEAD_DIM).astype(jnp.bfloat16)

        ones_image = jnp.ones((image_all, HEAD_DIM), jnp.bfloat16)
        ones_text = jnp.ones((text_all, HEAD_DIM), jnp.bfloat16)
        for p in range(2):
            tk_s[p] = rows(2 * p * text_dev, text_dev)
            tv_s[p, :, :HEAD_DIM] = rows((2 * p + 1) * text_dev, text_dev)
            tv_s[p, :, HEAD_DIM:] = ones_text
        base = 4 * text_dev
        q_s[...] = rows(base, image_dev)
        k_s[...] = rows(base + image_dev, image_dev)
        v_s[:, :HEAD_DIM] = rows(base + 2 * image_dev, image_dev)
        v_s[:, HEAD_DIM:] = ones_image

    factor = HEAD_DIM ** (-0.5) * LOG2E
    contract = (((1,), (1,)), ((), ()))
    start = pl.multiple_of(block * block_rows, 16)
    queries = q_s[pl.ds(start, block_rows), :]
    scores = lax.dot_general(queries, k_s[...], contract, preferred_element_type=jnp.float32)
    image_max = jnp.max(scores, axis=1, keepdims=True) * factor
    weights = jnp.exp2(scores * factor - image_max).astype(jnp.bfloat16)
    image_out = jnp.dot(weights, v_s[...], preferred_element_type=jnp.float32)
    for p in range(2):
        text = lax.dot_general(queries, tk_s[p], contract, preferred_element_type=jnp.float32)
        text = jnp.where(live_ref[0, p:p + 1, :] != 0, text * factor, -jnp.inf)
        pass_max = jnp.maximum(image_max, jnp.max(text, axis=1, keepdims=True))
        ratio = jnp.exp2(image_max - pass_max)
        text_weights = jnp.exp2(text - pass_max).astype(jnp.bfloat16)
        both = ratio * image_out + jnp.dot(text_weights, tv_s[p], preferred_element_type=jnp.float32)
        result = both[:, :HEAD_DIM] / both[:, HEAD_DIM:]
        out_ref[:, 0, p] = result.reshape(block_rows // image_dev, image_dev, HEAD_DIM).astype(out_ref.dtype)


def attend(gathered, live, image_dev, text_dev):
    sources, owned = gathered.shape[:2]
    rows = gathered.shape[2]
    image_all, text_all = sources * image_dev, sources * text_dev
    per_block = 4
    blocks = sources // per_block
    block_rows = per_block * image_dev
    scores_flops = 2 * image_all * (image_all + 2 * text_all) * HEAD_DIM
    return pl.pallas_call(
        functools.partial(attention_kernel, image_dev, text_dev, block_rows),
        grid=(owned, blocks),
        in_specs=[
            pl.BlockSpec((sources, 1, rows, HEAD_DIM), lambda j, i: (0, j, 0, 0)),
            pl.BlockSpec((1, 2, text_all), lambda j, i: (j, 0, 0)),
        ],
        out_specs=pl.BlockSpec((per_block, 1, 2, image_dev, HEAD_DIM), lambda j, i: (i, j, 0, 0, 0)),
        out_shape=jax.ShapeDtypeStruct((sources, owned, 2, image_dev, HEAD_DIM), jnp.bfloat16),
        scratch_shapes=[
            pltpu.VMEM((image_all, HEAD_DIM), jnp.bfloat16),
            pltpu.VMEM((image_all, HEAD_DIM), jnp.bfloat16),
            pltpu.VMEM((image_all, 2 * HEAD_DIM), jnp.bfloat16),
            pltpu.VMEM((2, text_all, HEAD_DIM), jnp.bfloat16),
            pltpu.VMEM((2, text_all, 2 * HEAD_DIM), jnp.bfloat16),
        ],
        compiler_params=pltpu.CompilerParams(
            dimension_semantics=("arbitrary", "arbitrary"), vmem_limit_bytes=48 << 20
        ),
        cost_estimate=pl.CostEstimate(
            flops=2 * owned * scores_flops,
            bytes_accessed=2 * gathered.size + 4 * owned * image_all * HEAD_DIM,
            transcendentals=owned * image_all * (image_all + 2 * text_all),
        ),
        name="attention",
    )(gathered, live)


def head_kernel(
    samples, image_dev, back_ref, frozen_ref, trainee_ref, states_ref, gate_ref, scale_ref, head_ref,
    cot_ref, att_ref, both_s, mixed_s, square_s,
):
    step = pl.program_id(0)
    rows = samples * image_dev
    width = frozen_ref.shape[1]

    @pl.when(step == 0)
    def _():
        for h in range(HEADS):
            for p in range(2):
                piece = back_ref[h, :, p].astype(jnp.float32).reshape(rows, HEAD_DIM)
                both_s[p * rows:(p + 1) * rows, h * HEAD_DIM:(h + 1) * HEAD_DIM] = piece.astype(jnp.bfloat16)
        square_s[...] = jnp.zeros_like(square_s)

    def spread(values):
        return jnp.concatenate(
            [jnp.broadcast_to(values[b:b + 1, :], (image_dev, values.shape[1])) for b in range(samples)], axis=0
        )

    columns = pl.ds(pl.multiple_of(step * width, 128), width)
    states = states_ref[:, :, columns].astype(jnp.float32).reshape(rows, width)
    gate = spread(gate_ref[:, columns])
    frozen = jnp.dot(both_s[...], frozen_ref[...], preferred_element_type=jnp.float32)
    trainee = jnp.dot(both_s[:rows, :], trainee_ref[...], preferred_element_type=jnp.float32)
    for k, branch in enumerate((frozen[:rows], frozen[rows:], trainee)):
        mixed = states + gate * branch
        mixed_s[k, :, columns] = mixed
        square = mixed * mixed
        total = square[:, :128]
        for c in range(1, width // 128):
            total = total + square[:, c * 128:(c + 1) * 128]
        square_s[k] += total

    @pl.when(step == pl.num_programs(0) - 1)
    def _():
        lift = 1.0 + spread(scale_ref[...])
        velocities = []
        for k in range(3):
            mean = jnp.sum(square_s[k], axis=1, keepdims=True) * (1.0 / WIDTH)
            root = lax.rsqrt(mean + 1e-06)
            normed = (mixed_s[k] * root * lift).astype(jnp.bfloat16)
            velocities.append(jnp.dot(normed, head_ref[...], preferred_element_type=jnp.float32))
        velocity_c, velocity_n, velocity_s = velocities
        target = velocity_n - (velocity_c - velocity_n)
        pull = (velocity_s - target) * (2.0 / SAMPLES)
        high = pull.astype(jnp.bfloat16)
        low = (pull - high.astype(jnp.float32)).astype(jnp.bfloat16)
        contract = (((1,), (1,)), ((), ()))
        inner = lax.dot_general(high, head_ref[...], contract, preferred_element_type=jnp.float32)
        inner += lax.dot_general(low, head_ref[...], contract, preferred_element_type=jnp.float32)
        inner = inner * lift
        mixed = mixed_s[2]
        along = jnp.sum(inner * mixed, axis=1, keepdims=True) * (1.0 / WIDTH)
        cot = root * inner - mixed * (root * root * root * along)
        cot_ref[...] = (cot * spread(gate_ref[...])).astype(cot_ref.dtype)
        att_ref[...] = both_s[:rows, :]


def project(back, frozen, trainee, states, gate, scale, final_head):
    samples, image_dev = states.shape[:2]
    rows = samples * image_dev
    inner = frozen.shape[0]
    width = 256
    whole = lambda shape: pl.BlockSpec(shape, lambda n: (0,) * len(shape))
    return pl.pallas_call(
        functools.partial(head_kernel, samples, image_dev),
        grid=(WIDTH // width,),
        in_specs=[
            whole(back.shape),
            pl.BlockSpec((inner, width), lambda n: (0, n)),
            pl.BlockSpec((inner, width), lambda n: (0, n)),
            whole(states.shape),
            whole(gate.shape),
            whole(scale.shape),
            whole(final_head.shape),
        ],
        out_specs=[whole((rows, WIDTH)), whole((rows, inner))],
        out_shape=[
            jax.ShapeDtypeStruct((rows, WIDTH), jnp.bfloat16),
            jax.ShapeDtypeStruct((rows, inner), jnp.bfloat16),
        ],
        scratch_shapes=[
            pltpu.VMEM((2 * rows, inner), jnp.bfloat16),
            pltpu.VMEM((3, rows, WIDTH), jnp.float32),
            pltpu.VMEM((3, rows, 128), jnp.float32),
        ],
        compiler_params=pltpu.CompilerParams(dimension_semantics=("arbitrary",), vmem_limit_bytes=40 << 20),
        cost_estimate=pl.CostEstimate(
            flops=6 * rows * inner * WIDTH,
            bytes_accessed=4 * inner * WIDTH + 4 * rows * inner,
            transcendentals=3 * rows,
        ),
        name="project",
    )(back, frozen, trainee, states, gate, scale, final_head)


def shards(
    image_qkv,
    text_kv,
    prompt_ids,
    timesteps,
    image_states,
    frozen_out,
    trainee_out,
    time_mod,
    final_head,
):
    group_size = lax.axis_size("seq")
    position = lax.axis_index("seq")
    image_dev = image_qkv.shape[3]
    text_dev = text_kv.shape[4]
    owned = SAMPLES * HEADS // group_size
    image_items = image_qkv.transpose(2, 1, 0, 3, 4).reshape(group_size, owned, 3 * image_dev, HEAD_DIM)
    text_items = text_kv.transpose(3, 2, 0, 1, 4, 5).reshape(group_size, owned, 4 * text_dev, HEAD_DIM)
    sample_of = (position * owned + jnp.arange(owned, dtype=jnp.int32)) % SAMPLES
    live = jnp.take(prompt_ids, sample_of, axis=1).transpose(1, 0, 2)
    live = (live != 0).astype(jnp.int32)
    half_dim = TIME_DIM // 2
    freqs = jnp.exp(-math.log(10000.0) * jnp.arange(half_dim, dtype=jnp.float32) / half_dim)
    angles = timesteps.astype(jnp.float32)[:, None] * freqs[None, :]
    embedding = jnp.concatenate([jnp.cos(angles), jnp.sin(angles)], 1)
    modulation = jnp.dot(embedding, time_mod.astype(jnp.float32), precision=lax.Precision.HIGHEST)
    gate = modulation[:, :WIDTH]
    scale = modulation[:, WIDTH:]
    chunks = CHUNKS if owned == SAMPLES else 1
    items = owned // chunks
    samples = SAMPLES // chunks
    exchange = functools.partial(lax.all_to_all, axis_name="seq", split_axis=0, concat_axis=0, tiled=True)
    gathered = []
    for c in range(chunks):
        own = slice(c * items, (c + 1) * items)
        gathered.append(exchange(jnp.concatenate([text_items[:, own], image_items[:, own]], axis=2)))
    all_frozen = lax.all_gather(frozen_out, "seq", axis=0, tiled=True)
    all_trainee = lax.all_gather(trainee_out, "seq", axis=0, tiled=True)
    cotangents, columns = [], []
    for c in range(chunks):
        both = attend(gathered[c], live[c * items:(c + 1) * items], image_dev, text_dev)
        back = exchange(both).reshape(HEADS, samples, 2, image_dev, HEAD_DIM)
        part = slice(c * samples, (c + 1) * samples)
        cot, att = project(
            back, all_frozen, all_trainee, image_states[part], gate[part], scale[part], final_head
        )
        cotangents.append(cot)
        columns.append(att)
    partial = lax.dot_general(
        jnp.concatenate(columns),
        jnp.concatenate(cotangents),
        (((0,), (0,)), ((), ())),
        preferred_element_type=jnp.float32,
    ).astype(jnp.bfloat16)
    total = lax.psum_scatter(partial, "seq", scatter_dimension=0, tiled=True)
    return total.astype(jnp.float32)


def solution(mesh):
    return jax.shard_map(
        shards,
        mesh=mesh,
        in_specs=(
            P(None, "grp", None, "seq", None),
            P(None, None, "grp", None, "seq", None),
            P(None, "grp", None),
            P("grp"),
            P("grp", "seq", None),
            P("seq", None),
            P(("grp", "seq"), None),
            P(),
            P(),
        ),
        out_specs=P(("grp", "seq"), None),
        check_vma=False,
    )
```

```python
import functools
import math

import jax
import jax.numpy as jnp
from jax import lax
from jax.experimental import pallas as pl
from jax.experimental.pallas import tpu as pltpu
from jax.sharding import PartitionSpec as P

SAMPLES = 4
HEADS = 16
HEAD_DIM = 128
WIDTH = 1536
TIME_DIM = 256
LOG2E = math.log2(math.e)


def attention_kernel(image_dev, text_dev, block_rows, x_ref, live_ref, out_ref, q_s, k_s, v_s, tk_s, tv_s):
    sources = x_ref.shape[0]
    image_all = sources * image_dev
    text_all = sources * text_dev
    block = pl.program_id(1)

    @pl.when(block == 0)
    def _():
        def rows(start, count):
            piece = x_ref[:, 0, start:start + count, :].astype(jnp.float32)
            return piece.reshape(sources * count, HEAD_DIM).astype(jnp.bfloat16)

        ones_image = jnp.ones((image_all, HEAD_DIM), jnp.bfloat16)
        ones_text = jnp.ones((text_all, HEAD_DIM), jnp.bfloat16)
        for p in range(2):
            tk_s[p] = rows(2 * p * text_dev, text_dev)
            tv_s[p, :, :HEAD_DIM] = rows((2 * p + 1) * text_dev, text_dev)
            tv_s[p, :, HEAD_DIM:] = ones_text
        base = 4 * text_dev
        q_s[...] = rows(base, image_dev)
        k_s[...] = rows(base + image_dev, image_dev)
        v_s[:, :HEAD_DIM] = rows(base + 2 * image_dev, image_dev)
        v_s[:, HEAD_DIM:] = ones_image

    factor = HEAD_DIM ** (-0.5) * LOG2E
    contract = (((1,), (1,)), ((), ()))
    start = pl.multiple_of(block * block_rows, 16)
    queries = q_s[pl.ds(start, block_rows), :]
    scores = lax.dot_general(queries, k_s[...], contract, preferred_element_type=jnp.float32)
    image_max = jnp.max(scores, axis=1, keepdims=True) * factor
    weights = jnp.exp2(scores * factor - image_max).astype(jnp.bfloat16)
    image_out = jnp.dot(weights, v_s[...], preferred_element_type=jnp.float32)
    for p in range(2):
        text = lax.dot_general(queries, tk_s[p], contract, preferred_element_type=jnp.float32)
        text = jnp.where(live_ref[0, p:p + 1, :] != 0, text * factor, -jnp.inf)
        pass_max = jnp.maximum(image_max, jnp.max(text, axis=1, keepdims=True))
        ratio = jnp.exp2(image_max - pass_max)
        text_weights = jnp.exp2(text - pass_max).astype(jnp.bfloat16)
        both = ratio * image_out + jnp.dot(text_weights, tv_s[p], preferred_element_type=jnp.float32)
        result = both[:, :HEAD_DIM] / both[:, HEAD_DIM:]
        out_ref[:, 0, p] = result.reshape(block_rows // image_dev, image_dev, HEAD_DIM).astype(out_ref.dtype)


def attend(gathered, live, image_dev, text_dev):
    sources, owned = gathered.shape[:2]
    rows = gathered.shape[2]
    image_all, text_all = sources * image_dev, sources * text_dev
    per_block = 4
    blocks = sources // per_block
    block_rows = per_block * image_dev
    scores_flops = 2 * image_all * (image_all + 2 * text_all) * HEAD_DIM
    return pl.pallas_call(
        functools.partial(attention_kernel, image_dev, text_dev, block_rows),
        grid=(owned, blocks),
        in_specs=[
            pl.BlockSpec((sources, 1, rows, HEAD_DIM), lambda j, i: (0, j, 0, 0)),
            pl.BlockSpec((1, 2, text_all), lambda j, i: (j, 0, 0)),
        ],
        out_specs=pl.BlockSpec((per_block, 1, 2, image_dev, HEAD_DIM), lambda j, i: (i, j, 0, 0, 0)),
        out_shape=jax.ShapeDtypeStruct((sources, owned, 2, image_dev, HEAD_DIM), jnp.bfloat16),
        scratch_shapes=[
            pltpu.VMEM((image_all, HEAD_DIM), jnp.bfloat16),
            pltpu.VMEM((image_all, HEAD_DIM), jnp.bfloat16),
            pltpu.VMEM((image_all, 2 * HEAD_DIM), jnp.bfloat16),
            pltpu.VMEM((2, text_all, HEAD_DIM), jnp.bfloat16),
            pltpu.VMEM((2, text_all, 2 * HEAD_DIM), jnp.bfloat16),
        ],
        compiler_params=pltpu.CompilerParams(
            dimension_semantics=("arbitrary", "arbitrary"), vmem_limit_bytes=48 << 20
        ),
        cost_estimate=pl.CostEstimate(
            flops=2 * owned * scores_flops,
            bytes_accessed=2 * gathered.size + 4 * owned * image_all * HEAD_DIM,
            transcendentals=owned * image_all * (image_all + 2 * text_all),
        ),
        name="attention",
    )(gathered, live)


def head_kernel(
    samples, image_dev, back_ref, frozen_ref, trainee_ref, states_ref, gate_ref, scale_ref, head_ref,
    cot_ref, att_ref, both_s, mixed_s, square_s,
):
    step = pl.program_id(0)
    rows = samples * image_dev
    width = frozen_ref.shape[1]

    @pl.when(step == 0)
    def _():
        for h in range(HEADS):
            for p in range(2):
                piece = back_ref[h, :, p].astype(jnp.float32).reshape(rows, HEAD_DIM)
                both_s[p * rows:(p + 1) * rows, h * HEAD_DIM:(h + 1) * HEAD_DIM] = piece.astype(jnp.bfloat16)
        square_s[...] = jnp.zeros_like(square_s)

    def spread(values):
        return jnp.concatenate(
            [jnp.broadcast_to(values[b:b + 1, :], (image_dev, values.shape[1])) for b in range(samples)], axis=0
        )

    columns = pl.ds(pl.multiple_of(step * width, 128), width)
    states = states_ref[:, :, columns].astype(jnp.float32).reshape(rows, width)
    gate = spread(gate_ref[:, columns])
    frozen = jnp.dot(both_s[...], frozen_ref[...], preferred_element_type=jnp.float32)
    trainee = jnp.dot(both_s[:rows, :], trainee_ref[...], preferred_element_type=jnp.float32)
    for k, branch in enumerate((frozen[:rows], frozen[rows:], trainee)):
        mixed = states + gate * branch
        mixed_s[k, :, columns] = mixed
        square = mixed * mixed
        total = square[:, :128]
        for c in range(1, width // 128):
            total = total + square[:, c * 128:(c + 1) * 128]
        square_s[k] += total

    @pl.when(step == pl.num_programs(0) - 1)
    def _():
        lift = 1.0 + spread(scale_ref[...])
        velocities = []
        for k in range(3):
            mean = jnp.sum(square_s[k], axis=1, keepdims=True) * (1.0 / WIDTH)
            root = lax.rsqrt(mean + 1e-06)
            normed = (mixed_s[k] * root * lift).astype(jnp.bfloat16)
            velocities.append(jnp.dot(normed, head_ref[...], preferred_element_type=jnp.float32))
        velocity_c, velocity_n, velocity_s = velocities
        target = velocity_n - (velocity_c - velocity_n)
        pull = (velocity_s - target) * (2.0 / SAMPLES)
        high = pull.astype(jnp.bfloat16)
        low = (pull - high.astype(jnp.float32)).astype(jnp.bfloat16)
        contract = (((1,), (1,)), ((), ()))
        inner = lax.dot_general(high, head_ref[...], contract, preferred_element_type=jnp.float32)
        inner += lax.dot_general(low, head_ref[...], contract, preferred_element_type=jnp.float32)
        inner = inner * lift
        mixed = mixed_s[2]
        along = jnp.sum(inner * mixed, axis=1, keepdims=True) * (1.0 / WIDTH)
        cot = root * inner - mixed * (root * root * root * along)
        cot_ref[...] = (cot * spread(gate_ref[...])).astype(cot_ref.dtype)
        for h in range(HEADS):
            att_ref[h] = both_s[:rows, h * HEAD_DIM:(h + 1) * HEAD_DIM]


def project(back, frozen, trainee, states, gate, scale, final_head):
    samples, image_dev = states.shape[:2]
    rows = samples * image_dev
    inner = frozen.shape[0]
    width = 256
    whole = lambda shape: pl.BlockSpec(shape, lambda n: (0,) * len(shape))
    return pl.pallas_call(
        functools.partial(head_kernel, samples, image_dev),
        grid=(WIDTH // width,),
        in_specs=[
            whole(back.shape),
            pl.BlockSpec((inner, width), lambda n: (0, n)),
            pl.BlockSpec((inner, width), lambda n: (0, n)),
            whole(states.shape),
            whole(gate.shape),
            whole(scale.shape),
            whole(final_head.shape),
        ],
        out_specs=[whole((rows, WIDTH)), whole((HEADS, rows, HEAD_DIM))],
        out_shape=[
            jax.ShapeDtypeStruct((rows, WIDTH), jnp.bfloat16),
            jax.ShapeDtypeStruct((HEADS, rows, HEAD_DIM), jnp.bfloat16),
        ],
        scratch_shapes=[
            pltpu.VMEM((2 * rows, inner), jnp.bfloat16),
            pltpu.VMEM((3, rows, WIDTH), jnp.float32),
            pltpu.VMEM((3, rows, 128), jnp.float32),
        ],
        compiler_params=pltpu.CompilerParams(dimension_semantics=("arbitrary",), vmem_limit_bytes=60 << 20),
        cost_estimate=pl.CostEstimate(
            flops=6 * rows * inner * WIDTH,
            bytes_accessed=4 * inner * WIDTH + 4 * rows * inner,
            transcendentals=3 * rows,
        ),
        name="project",
    )(back, frozen, trainee, states, gate, scale, final_head)


def product_kernel(mine, peer, att_ref, att_peer_ref, cot_ref, cot_peer_ref, *out_refs):
    half = WIDTH // 2
    slots = out_refs[0].shape[0]
    for part, out_ref in enumerate(out_refs):
        picked = range(part * slots, (part + 1) * slots)
        own = jnp.concatenate([att_ref[mine[i]] for i in picked], axis=1)
        other = jnp.concatenate([att_peer_ref[peer[i]] for i in picked], axis=1)
        columns = slice(part * half, (part + 1) * half)
        contract = (((0,), (0,)), ((), ()))
        total = lax.dot_general(
            jnp.concatenate([own, other], axis=0),
            jnp.concatenate([cot_ref[:, columns], cot_peer_ref[:, columns]], axis=0),
            contract,
            preferred_element_type=jnp.float32,
        )
        out_ref[...] = total.reshape(out_ref.shape).astype(out_ref.dtype)


def product(blocks, core, att, att_peer, cot, cot_peer):
    slots = blocks.shape[0] // 2
    rows = cot.shape[0]
    half = WIDTH // 2
    out = jax.ShapeDtypeStruct((slots, HEAD_DIM, half), jnp.bfloat16)
    return pl.pallas_call(
        product_kernel,
        in_specs=[pl.BlockSpec(memory_space=pltpu.SMEM)] * 2 + [pl.BlockSpec(memory_space=pltpu.VMEM)] * 4,
        out_specs=[pl.BlockSpec(memory_space=pltpu.VMEM)] * 2,
        out_shape=[out, out],
        compiler_params=pltpu.CompilerParams(vmem_limit_bytes=32 << 20),
        cost_estimate=pl.CostEstimate(
            flops=8 * slots * rows * HEAD_DIM * half,
            bytes_accessed=4 * rows * (WIDTH + 2 * slots * HEAD_DIM) + 4 * slots * HEAD_DIM * half,
            transcendentals=0,
        ),
        name="product",
    )(2 * blocks + core, blocks, att, att_peer, cot, cot_peer)


def reduce_by_halving(att, cot, position, group_size):
    levels = group_size.bit_length() - 1
    chips = group_size // 2
    bit = [(position >> k) & 1 for k in range(levels)]

    def swap(x, k):
        return lax.ppermute(x, "seq", [(s, s ^ (1 << k)) for s in range(group_size)])

    by_core = att.reshape(chips, 2, *att.shape[1:])
    cot_peer = swap(cot, 0)
    att_peer = swap(lax.dynamic_index_in_dim(by_core, 1 - bit[0], 1, keepdims=False), 0)
    orders = (tuple(range(1, levels)), tuple(range(2, levels)) + (1,))

    def chip_blocks(keep):
        tables = []
        for order in orders:
            k = order[0] - 1
            ids = [m for m in range(chips) if not (m >> k) & 1]
            wanted = bit[order[0]] if keep else 1 - bit[order[0]]
            tables.append(jnp.array(ids, jnp.int32) + (wanted << k))
        return jnp.concatenate(tables)

    factors = (bit[0], att, att_peer, cot, cot_peer)
    sent = product(chip_blocks(False), *factors)
    kept = product(chip_blocks(True), *factors)
    state = []
    for part, order in enumerate(orders):
        left = sorted(order[1:], reverse=True)
        shape = (2,) * len(left) + (HEAD_DIM, WIDTH // 2)
        state.append((kept[part].reshape(shape), swap(sent[part], order[0]).reshape(shape), left))
    for level in range(1, levels - 1):
        following = []
        for (keep, got, left), order in zip(state, orders):
            k = order[level]
            axis = left.index(k)

            def half(x, which):
                return lax.dynamic_index_in_dim(x, which, axis, keepdims=False).astype(jnp.float32)

            def joined(which):
                return (half(keep, which) + half(got, which)).astype(jnp.bfloat16)

            following.append((joined(bit[k]), swap(joined(1 - bit[k]), k), [n for n in left if n != k]))
        state = following
    return jnp.concatenate([keep.astype(jnp.float32) + got.astype(jnp.float32) for keep, got, _ in state], axis=1)


def shards(
    image_qkv,
    text_kv,
    prompt_ids,
    timesteps,
    image_states,
    frozen_out,
    trainee_out,
    time_mod,
    final_head,
):
    group_size = lax.axis_size("seq")
    position = lax.axis_index("seq")
    image_dev = image_qkv.shape[3]
    text_dev = text_kv.shape[4]
    owned = SAMPLES * HEADS // group_size
    image_items = image_qkv.transpose(2, 1, 0, 3, 4).reshape(group_size, owned, 3 * image_dev, HEAD_DIM)
    text_items = text_kv.transpose(3, 2, 0, 1, 4, 5).reshape(group_size, owned, 4 * text_dev, HEAD_DIM)
    sample_of = (position * owned + jnp.arange(owned, dtype=jnp.int32)) % SAMPLES
    live = jnp.take(prompt_ids, sample_of, axis=1).transpose(1, 0, 2)
    live = (live != 0).astype(jnp.int32)
    half_dim = TIME_DIM // 2
    freqs = jnp.exp(-math.log(10000.0) * jnp.arange(half_dim, dtype=jnp.float32) / half_dim)
    angles = timesteps.astype(jnp.float32)[:, None] * freqs[None, :]
    embedding = jnp.concatenate([jnp.cos(angles), jnp.sin(angles)], 1)
    modulation = jnp.dot(embedding, time_mod.astype(jnp.float32), precision=lax.Precision.HIGHEST)
    gate = modulation[:, :WIDTH]
    scale = modulation[:, WIDTH:]
    exchange = functools.partial(lax.all_to_all, axis_name="seq", split_axis=0, concat_axis=0, tiled=True)
    gathered = exchange(jnp.concatenate([text_items, image_items], axis=2))
    all_frozen = lax.all_gather(frozen_out, "seq", axis=0, tiled=True)
    all_trainee = lax.all_gather(trainee_out, "seq", axis=0, tiled=True)
    both = attend(gathered, live, image_dev, text_dev)
    back = exchange(both).reshape(HEADS, SAMPLES, 2, image_dev, HEAD_DIM)
    cot, att = project(back, all_frozen, all_trainee, image_states, gate, scale, final_head)
    if group_size == HEADS:
        return reduce_by_halving(att, cot, position, group_size)
    partial = jnp.einsum("hrd,rc->hdc", att, cot, preferred_element_type=jnp.float32)
    partial = partial.reshape(HEADS * HEAD_DIM, WIDTH).astype(jnp.bfloat16)
    return lax.psum_scatter(partial, "seq", scatter_dimension=0, tiled=True).astype(jnp.float32)


def solution(mesh):
    return jax.shard_map(
        shards,
        mesh=mesh,
        in_specs=(
            P(None, "grp", None, "seq", None),
            P(None, None, "grp", None, "seq", None),
            P(None, "grp", None),
            P("grp"),
            P("grp", "seq", None),
            P("seq", None),
            P(("grp", "seq"), None),
            P(),
            P(),
        ),
        out_specs=P(("grp", "seq"), None),
        check_vma=False,
    )
```

```python
import functools
import math

import jax
import jax.numpy as jnp
from jax import lax
from jax.experimental import pallas as pl
from jax.experimental.pallas import tpu as pltpu
from jax.sharding import PartitionSpec as P

SAMPLES = 4
HEADS = 16
HEAD_DIM = 128
WIDTH = 1536
TIME_DIM = 256
WAVES = 2
VMEM_PRODUCT = 60 << 20
LOG2E = math.log2(math.e)


def attention_kernel(image_dev, text_dev, block_rows, x_ref, live_ref, out_ref, q_s, k_s, v_s, tk_s, tv_s):
    sources = x_ref.shape[0]
    image_all = sources * image_dev
    text_all = sources * text_dev
    block = pl.program_id(1)

    @pl.when(block == 0)
    def _():
        def rows(start, count):
            piece = x_ref[:, 0, start:start + count, :].astype(jnp.float32)
            return piece.reshape(sources * count, HEAD_DIM).astype(jnp.bfloat16)

        ones_image = jnp.ones((image_all, HEAD_DIM), jnp.bfloat16)
        ones_text = jnp.ones((text_all, HEAD_DIM), jnp.bfloat16)
        for p in range(2):
            tk_s[p] = rows(2 * p * text_dev, text_dev)
            tv_s[p, :, :HEAD_DIM] = rows((2 * p + 1) * text_dev, text_dev)
            tv_s[p, :, HEAD_DIM:] = ones_text
        base = 4 * text_dev
        q_s[...] = rows(base, image_dev)
        k_s[...] = rows(base + image_dev, image_dev)
        v_s[:, :HEAD_DIM] = rows(base + 2 * image_dev, image_dev)
        v_s[:, HEAD_DIM:] = ones_image

    factor = HEAD_DIM ** (-0.5) * LOG2E
    contract = (((1,), (1,)), ((), ()))
    start = pl.multiple_of(block * block_rows, 16)
    queries = q_s[pl.ds(start, block_rows), :]
    scores = lax.dot_general(queries, k_s[...], contract, preferred_element_type=jnp.float32)
    image_max = jnp.max(scores, axis=1, keepdims=True) * factor
    weights = jnp.exp2(scores * factor - image_max).astype(jnp.bfloat16)
    image_out = jnp.dot(weights, v_s[...], preferred_element_type=jnp.float32)
    for p in range(2):
        text = lax.dot_general(queries, tk_s[p], contract, preferred_element_type=jnp.float32)
        text = jnp.where(live_ref[0, p:p + 1, :] != 0, text * factor, -jnp.inf)
        pass_max = jnp.maximum(image_max, jnp.max(text, axis=1, keepdims=True))
        ratio = jnp.exp2(image_max - pass_max)
        text_weights = jnp.exp2(text - pass_max).astype(jnp.bfloat16)
        both = ratio * image_out + jnp.dot(text_weights, tv_s[p], preferred_element_type=jnp.float32)
        result = both[:, :HEAD_DIM] / both[:, HEAD_DIM:]
        out_ref[:, 0, p] = result.reshape(block_rows // image_dev, image_dev, HEAD_DIM).astype(out_ref.dtype)


def attend(gathered, live, image_dev, text_dev):
    sources, owned = gathered.shape[:2]
    rows = gathered.shape[2]
    image_all, text_all = sources * image_dev, sources * text_dev
    per_block = 4
    blocks = sources // per_block
    block_rows = per_block * image_dev
    scores_flops = 2 * image_all * (image_all + 2 * text_all) * HEAD_DIM
    return pl.pallas_call(
        functools.partial(attention_kernel, image_dev, text_dev, block_rows),
        grid=(owned, blocks),
        in_specs=[
            pl.BlockSpec((sources, 1, rows, HEAD_DIM), lambda j, i: (0, j, 0, 0)),
            pl.BlockSpec((1, 2, text_all), lambda j, i: (j, 0, 0)),
        ],
        out_specs=pl.BlockSpec((per_block, 1, 2, image_dev, HEAD_DIM), lambda j, i: (i, j, 0, 0, 0)),
        out_shape=jax.ShapeDtypeStruct((sources, owned, 2, image_dev, HEAD_DIM), jnp.bfloat16),
        scratch_shapes=[
            pltpu.VMEM((image_all, HEAD_DIM), jnp.bfloat16),
            pltpu.VMEM((image_all, HEAD_DIM), jnp.bfloat16),
            pltpu.VMEM((image_all, 2 * HEAD_DIM), jnp.bfloat16),
            pltpu.VMEM((2, text_all, HEAD_DIM), jnp.bfloat16),
            pltpu.VMEM((2, text_all, 2 * HEAD_DIM), jnp.bfloat16),
        ],
        compiler_params=pltpu.CompilerParams(
            dimension_semantics=("arbitrary", "arbitrary"), vmem_limit_bytes=48 << 20
        ),
        cost_estimate=pl.CostEstimate(
            flops=2 * owned * scores_flops,
            bytes_accessed=2 * gathered.size + 4 * owned * image_all * HEAD_DIM,
            transcendentals=owned * image_all * (image_all + 2 * text_all),
        ),
        name="attention",
    )(gathered, live)


def head_kernel(
    samples, image_dev, blocks_ref, back_ref, frozen_ref, frozen_other_ref, trainee_ref, states_ref, gate_ref,
    scale_ref, head_ref, cot_ref, att_ref, both_s, mixed_s, square_s,
):
    step = pl.program_id(0)
    rows = samples * image_dev
    width = frozen_ref.shape[1]

    @pl.when(step == 0)
    def _():
        for h in range(HEADS):
            for p in range(2):
                piece = back_ref[h, :, p].astype(jnp.float32).reshape(rows, HEAD_DIM)
                both_s[p * rows:(p + 1) * rows, h * HEAD_DIM:(h + 1) * HEAD_DIM] = piece.astype(jnp.bfloat16)
        square_s[...] = jnp.zeros_like(square_s)

    def spread(values):
        return jnp.concatenate(
            [jnp.broadcast_to(values[b:b + 1, :], (image_dev, values.shape[1])) for b in range(samples)], axis=0
        )

    columns = pl.ds(pl.multiple_of(blocks_ref[step] * width, 128), width)
    states = states_ref[:, :, columns].astype(jnp.float32).reshape(rows, width)
    gate = spread(gate_ref[:, columns])
    weights = jnp.where(step < pl.num_programs(0) // 2, frozen_ref[...], frozen_other_ref[...])
    frozen = jnp.dot(both_s[...], weights, preferred_element_type=jnp.float32)
    trainee = jnp.dot(both_s[:rows, :], trainee_ref[...], preferred_element_type=jnp.float32)
    for k, branch in enumerate((frozen[:rows], frozen[rows:], trainee)):
        mixed = states + gate * branch
        mixed_s[k, :, columns] = mixed
        square = mixed * mixed
        total = square[:, :128]
        for c in range(1, width // 128):
            total = total + square[:, c * 128:(c + 1) * 128]
        square_s[k] += total

    @pl.when(step == pl.num_programs(0) - 1)
    def _():
        lift = 1.0 + spread(scale_ref[...])
        velocities = []
        for k in range(3):
            mean = jnp.sum(square_s[k], axis=1, keepdims=True) * (1.0 / WIDTH)
            root = lax.rsqrt(mean + 1e-06)
            normed = (mixed_s[k] * root * lift).astype(jnp.bfloat16)
            velocities.append(jnp.dot(normed, head_ref[...], preferred_element_type=jnp.float32))
        velocity_c, velocity_n, velocity_s = velocities
        target = velocity_n - (velocity_c - velocity_n)
        pull = (velocity_s - target) * (2.0 / SAMPLES)
        high = pull.astype(jnp.bfloat16)
        low = (pull - high.astype(jnp.float32)).astype(jnp.bfloat16)
        contract = (((1,), (1,)), ((), ()))
        inner = lax.dot_general(high, head_ref[...], contract, preferred_element_type=jnp.float32)
        inner += lax.dot_general(low, head_ref[...], contract, preferred_element_type=jnp.float32)
        inner = inner * lift
        mixed = mixed_s[2]
        along = jnp.sum(inner * mixed, axis=1, keepdims=True) * (1.0 / WIDTH)
        cot = root * inner - mixed * (root * root * root * along)
        cot_ref[...] = (cot * spread(gate_ref[...])).astype(cot_ref.dtype)
        for h in range(HEADS):
            att_ref[h] = both_s[:rows, h * HEAD_DIM:(h + 1) * HEAD_DIM]


def project(back, half, frozen, frozen_other, trainee, states, gate, scale, final_head):
    samples, image_dev = states.shape[:2]
    rows = samples * image_dev
    inner = trainee.shape[0]
    width = 256
    steps = WIDTH // width
    blocks = (jnp.arange(steps, dtype=jnp.int32) + half * (steps // 2)) % steps
    whole = lambda shape: pl.BlockSpec(shape, lambda n, blocks: (0,) * len(shape))
    return pl.pallas_call(
        functools.partial(head_kernel, samples, image_dev),
        grid_spec=pltpu.PrefetchScalarGridSpec(
            num_scalar_prefetch=1,
            grid=(steps,),
            in_specs=[
                whole(back.shape),
                pl.BlockSpec((inner, width), lambda n, blocks: (0, jnp.minimum(n, steps // 2 - 1))),
                pl.BlockSpec((inner, width), lambda n, blocks: (0, jnp.maximum(n - steps // 2, 0))),
                pl.BlockSpec((inner, width), lambda n, blocks: (0, blocks[n])),
                whole(states.shape),
                whole(gate.shape),
                whole(scale.shape),
                whole(final_head.shape),
            ],
            out_specs=[whole((rows, WIDTH)), whole((HEADS, rows, HEAD_DIM))],
            scratch_shapes=[
                pltpu.VMEM((2 * rows, inner), jnp.bfloat16),
                pltpu.VMEM((3, rows, WIDTH), jnp.float32),
                pltpu.VMEM((3, rows, 128), jnp.float32),
            ],
        ),
        out_shape=[
            jax.ShapeDtypeStruct((rows, WIDTH), jnp.bfloat16),
            jax.ShapeDtypeStruct((HEADS, rows, HEAD_DIM), jnp.bfloat16),
        ],
        compiler_params=pltpu.CompilerParams(dimension_semantics=("arbitrary",), vmem_limit_bytes=60 << 20),
        cost_estimate=pl.CostEstimate(
            flops=6 * rows * inner * WIDTH,
            bytes_accessed=4 * inner * WIDTH + 4 * rows * inner,
            transcendentals=3 * rows,
        ),
        name="project",
    )(blocks, back, frozen, frozen_other, trainee, states, gate, scale, final_head)


def product_kernel(first, mine, peer, att_ref, att_peer_ref, cot_ref, cot_peer_ref, *out_refs):
    slots, _, width = out_refs[0].shape
    for part, out_ref in enumerate(out_refs):
        picked = range(part * slots, (part + 1) * slots)
        own = jnp.concatenate([att_ref[mine[i]] for i in picked], axis=1)
        other = jnp.concatenate([att_peer_ref[peer[i]] for i in picked], axis=1)
        start = first + part * (WIDTH // 2)
        columns = slice(start, start + width)
        total = lax.dot_general(
            jnp.concatenate([own, other], axis=0),
            jnp.concatenate([cot_ref[:, columns], cot_peer_ref[:, columns]], axis=0),
            (((0,), (0,)), ((), ())),
            preferred_element_type=jnp.float32,
        )
        out_ref[...] = total.reshape(out_ref.shape).astype(out_ref.dtype)


def product(first, width, blocks, core, att, att_peer, cot, cot_peer):
    slots = blocks.shape[0] // 2
    rows = cot.shape[0]
    out = jax.ShapeDtypeStruct((slots, HEAD_DIM, width), jnp.bfloat16)
    return pl.pallas_call(
        functools.partial(product_kernel, first),
        in_specs=[pl.BlockSpec(memory_space=pltpu.SMEM)] * 2 + [pl.BlockSpec()] * 4,
        out_specs=[pl.BlockSpec()] * 2,
        out_shape=[out, out],
        compiler_params=pltpu.CompilerParams(vmem_limit_bytes=VMEM_PRODUCT),
        cost_estimate=pl.CostEstimate(
            flops=8 * slots * rows * HEAD_DIM * width,
            bytes_accessed=4 * rows * (WIDTH + 2 * slots * HEAD_DIM) + 4 * slots * HEAD_DIM * width,
            transcendentals=0,
        ),
        name="product",
    )(2 * blocks + core, blocks, att, att_peer, cot, cot_peer)


def reduce_by_halving(att, cot, position, group_size):
    levels = group_size.bit_length() - 1
    chips = group_size // 2
    width = WIDTH // 2 // WAVES
    bit = [(position >> k) & 1 for k in range(levels)]

    def swap(x, k):
        return lax.ppermute(x, "seq", [(s, s ^ (1 << k)) for s in range(group_size)])

    by_core = att.reshape(chips, 2, *att.shape[1:])
    cot_peer = swap(cot, 0)
    att_peer = swap(lax.dynamic_index_in_dim(by_core, 1 - bit[0], 1, keepdims=False), 0)
    orders = (tuple(range(1, levels)), tuple(range(2, levels)) + (1,))

    def chip_blocks(keep):
        tables = []
        for order in orders:
            k = order[0] - 1
            ids = [m for m in range(chips) if not (m >> k) & 1]
            wanted = bit[order[0]] if keep else 1 - bit[order[0]]
            tables.append(jnp.array(ids, jnp.int32) + (wanted << k))
        return jnp.concatenate(tables)

    factors = (bit[0], att, att_peer, cot, cot_peer)
    state = {}
    arrived = {}
    for wave in range(WAVES):
        sent = product(wave * width, width, chip_blocks(False), *factors)
        for part, order in enumerate(orders):
            arrived[wave, part] = swap(sent[part], order[0])
    for wave in range(WAVES):
        kept = product(wave * width, width, chip_blocks(True), *factors)
        for part, order in enumerate(orders):
            left = sorted(order[1:], reverse=True)
            shape = (2,) * len(left) + (HEAD_DIM, width)
            state[wave, part] = (kept[part].reshape(shape), arrived[wave, part].reshape(shape), left)
    for level in range(1, levels - 1):
        for wave in range(WAVES):
            for part, order in enumerate(orders):
                keep, got, left = state[wave, part]
                k = order[level]
                axis = left.index(k)

                def half(x, which):
                    return lax.dynamic_index_in_dim(x, which, axis, keepdims=False).astype(jnp.float32)

                def joined(which):
                    return (half(keep, which) + half(got, which)).astype(jnp.bfloat16)

                rest = [n for n in left if n != k]
                state[wave, part] = (joined(bit[k]), swap(joined(1 - bit[k]), k), rest)
    total = []
    for part in range(2):
        for wave in range(WAVES):
            keep, got, _ = state[wave, part]
            total.append(keep.astype(jnp.float32) + got.astype(jnp.float32))
    return jnp.concatenate(total, axis=1)


def shards(
    image_qkv,
    text_kv,
    prompt_ids,
    timesteps,
    image_states,
    frozen_out,
    trainee_out,
    time_mod,
    final_head,
):
    group_size = lax.axis_size("seq")
    position = lax.axis_index("seq")
    image_dev = image_qkv.shape[3]
    text_dev = text_kv.shape[4]
    owned = SAMPLES * HEADS // group_size
    image_items = image_qkv.transpose(2, 1, 0, 3, 4).reshape(group_size, owned, 3 * image_dev, HEAD_DIM)
    text_items = text_kv.transpose(3, 2, 0, 1, 4, 5).reshape(group_size, owned, 4 * text_dev, HEAD_DIM)
    sample_of = (position * owned + jnp.arange(owned, dtype=jnp.int32)) % SAMPLES
    live = jnp.take(prompt_ids, sample_of, axis=1).transpose(1, 0, 2)
    live = (live != 0).astype(jnp.int32)
    half_dim = TIME_DIM // 2
    freqs = jnp.exp(-math.log(10000.0) * jnp.arange(half_dim, dtype=jnp.float32) / half_dim)
    angles = timesteps.astype(jnp.float32)[:, None] * freqs[None, :]
    embedding = jnp.concatenate([jnp.cos(angles), jnp.sin(angles)], 1)
    modulation = jnp.dot(embedding, time_mod.astype(jnp.float32), precision=lax.Precision.HIGHEST)
    gate = modulation[:, :WIDTH]
    scale = modulation[:, WIDTH:]
    exchange = functools.partial(lax.all_to_all, axis_name="seq", split_axis=0, concat_axis=0, tiled=True)
    gathered = exchange(jnp.concatenate([text_items, image_items], axis=2))
    groups = lax.axis_size("grp")
    half = lax.axis_index("grp") % 2
    frozen = lax.all_gather(
        lax.dynamic_slice_in_dim(frozen_out, half * (WIDTH // 2), WIDTH // 2, axis=1), "seq", axis=0, tiled=True
    )
    gathered, frozen, trainee_out = lax.optimization_barrier((gathered, frozen, trainee_out))
    frozen_other = lax.ppermute(frozen, "grp", [(g, g ^ 1) for g in range(groups)])
    all_trainee = lax.all_gather(trainee_out, "seq", axis=0, tiled=True)
    both = attend(gathered, live, image_dev, text_dev)
    back = exchange(both).reshape(HEADS, SAMPLES, 2, image_dev, HEAD_DIM)
    cot, att = project(back, half, frozen, frozen_other, all_trainee, image_states, gate, scale, final_head)
    if group_size == HEADS:
        return reduce_by_halving(att, cot, position, group_size)
    partial = jnp.einsum("hrd,rc->hdc", att, cot, preferred_element_type=jnp.float32)
    partial = partial.reshape(HEADS * HEAD_DIM, WIDTH).astype(jnp.bfloat16)
    return lax.psum_scatter(partial, "seq", scatter_dimension=0, tiled=True).astype(jnp.float32)


def solution(mesh):
    return jax.shard_map(
        shards,
        mesh=mesh,
        in_specs=(
            P(None, "grp", None, "seq", None),
            P(None, None, "grp", None, "seq", None),
            P(None, "grp", None),
            P("grp"),
            P("grp", "seq", None),
            P("seq", None),
            P(("grp", "seq"), None),
            P(),
            P(),
        ),
        out_specs=P(("grp", "seq"), None),
        check_vma=False,
    )
```

```python
import functools
import math

import jax
import jax.numpy as jnp
from jax import lax
from jax.experimental import pallas as pl
from jax.experimental.pallas import tpu as pltpu
from jax.sharding import PartitionSpec as P

SAMPLES = 4
HEADS = 16
HEAD_DIM = 128
WIDTH = 1536
TIME_DIM = 256
WAVES = 2
VMEM_PRODUCT = 60 << 20
LOG2E = math.log2(math.e)


def attention_kernel(image_dev, text_dev, block_rows, x_ref, live_ref, out_ref, q_s, k_s, v_s, tk_s, tv_s):
    sources = x_ref.shape[0]
    image_all = sources * image_dev
    text_all = sources * text_dev
    block = pl.program_id(1)

    @pl.when(block == 0)
    def _():
        def rows(start, count):
            piece = x_ref[:, 0, start:start + count, :].astype(jnp.float32)
            return piece.reshape(sources * count, HEAD_DIM).astype(jnp.bfloat16)

        ones_image = jnp.ones((image_all, HEAD_DIM), jnp.bfloat16)
        ones_text = jnp.ones((text_all, HEAD_DIM), jnp.bfloat16)
        for p in range(2):
            tk_s[p] = rows(2 * p * text_dev, text_dev)
            tv_s[p, :, :HEAD_DIM] = rows((2 * p + 1) * text_dev, text_dev)
            tv_s[p, :, HEAD_DIM:] = ones_text
        base = 4 * text_dev
        q_s[...] = rows(base, image_dev)
        k_s[...] = rows(base + image_dev, image_dev)
        v_s[:, :HEAD_DIM] = rows(base + 2 * image_dev, image_dev)
        v_s[:, HEAD_DIM:] = ones_image

    factor = HEAD_DIM ** (-0.5) * LOG2E
    contract = (((1,), (1,)), ((), ()))
    start = pl.multiple_of(block * block_rows, 16)
    queries = q_s[pl.ds(start, block_rows), :]
    scores = lax.dot_general(queries, k_s[...], contract, preferred_element_type=jnp.float32)
    image_max = jnp.max(scores, axis=1, keepdims=True) * factor
    weights = jnp.exp2(scores * factor - image_max).astype(jnp.bfloat16)
    image_out = jnp.dot(weights, v_s[...], preferred_element_type=jnp.float32)
    for p in range(2):
        text = lax.dot_general(queries, tk_s[p], contract, preferred_element_type=jnp.float32)
        text = jnp.where(live_ref[0, p:p + 1, :] != 0, text * factor, -jnp.inf)
        pass_max = jnp.maximum(image_max, jnp.max(text, axis=1, keepdims=True))
        ratio = jnp.exp2(image_max - pass_max)
        text_weights = jnp.exp2(text - pass_max).astype(jnp.bfloat16)
        both = ratio * image_out + jnp.dot(text_weights, tv_s[p], preferred_element_type=jnp.float32)
        result = both[:, :HEAD_DIM] / both[:, HEAD_DIM:]
        out_ref[:, 0, p] = result.reshape(block_rows // image_dev, image_dev, HEAD_DIM).astype(out_ref.dtype)


def attend(gathered, live, image_dev, text_dev):
    sources, owned = gathered.shape[:2]
    rows = gathered.shape[2]
    image_all, text_all = sources * image_dev, sources * text_dev
    per_block = 4
    blocks = sources // per_block
    block_rows = per_block * image_dev
    scores_flops = 2 * image_all * (image_all + 2 * text_all) * HEAD_DIM
    return pl.pallas_call(
        functools.partial(attention_kernel, image_dev, text_dev, block_rows),
        grid=(owned, blocks),
        in_specs=[
            pl.BlockSpec((sources, 1, rows, HEAD_DIM), lambda j, i: (0, j, 0, 0)),
            pl.BlockSpec((1, 2, text_all), lambda j, i: (j, 0, 0)),
        ],
        out_specs=pl.BlockSpec((per_block, 1, 2, image_dev, HEAD_DIM), lambda j, i: (i, j, 0, 0, 0)),
        out_shape=jax.ShapeDtypeStruct((sources, owned, 2, image_dev, HEAD_DIM), jnp.bfloat16),
        scratch_shapes=[
            pltpu.VMEM((image_all, HEAD_DIM), jnp.bfloat16),
            pltpu.VMEM((image_all, HEAD_DIM), jnp.bfloat16),
            pltpu.VMEM((image_all, 2 * HEAD_DIM), jnp.bfloat16),
            pltpu.VMEM((2, text_all, HEAD_DIM), jnp.bfloat16),
            pltpu.VMEM((2, text_all, 2 * HEAD_DIM), jnp.bfloat16),
        ],
        compiler_params=pltpu.CompilerParams(
            dimension_semantics=("arbitrary", "arbitrary"), vmem_limit_bytes=48 << 20
        ),
        cost_estimate=pl.CostEstimate(
            flops=2 * owned * scores_flops,
            bytes_accessed=2 * gathered.size + 4 * owned * image_all * HEAD_DIM,
            transcendentals=owned * image_all * (image_all + 2 * text_all),
        ),
        name="attention",
    )(gathered, live)


def head_kernel(
    samples, image_dev, pieces, heads, back_ref, states_ref, gate_ref, scale_ref, head_ref, *refs,
):
    frozen_refs, trainee_refs = refs[:pieces], refs[pieces:2 * pieces]
    cot_ref, att_ref, both_s, mixed_s, square_s = refs[2 * pieces:]
    step = pl.program_id(0)
    rows = samples * image_dev
    width = frozen_refs[0].shape[1]

    @pl.when(step == 0)
    def _():
        for k in range(HEADS):
            h = heads[k]
            for p in range(2):
                piece = back_ref[h, :, p].astype(jnp.float32).reshape(rows, HEAD_DIM).astype(jnp.bfloat16)
                both_s[p * rows:(p + 1) * rows, k * HEAD_DIM:(k + 1) * HEAD_DIM] = piece
                if p == 0:
                    att_ref[h] = piece
        square_s[...] = jnp.zeros_like(square_s)

    def spread(values):
        return jnp.concatenate(
            [jnp.broadcast_to(values[b:b + 1, :], (image_dev, values.shape[1])) for b in range(samples)], axis=0
        )

    def times(count, weight_refs):
        weights = jnp.concatenate([weight_ref[...] for weight_ref in weight_refs], axis=0)
        return jnp.dot(both_s[:count, :], weights, preferred_element_type=jnp.float32)

    columns = pl.ds(pl.multiple_of(step * width, 128), width)
    states = states_ref[:, :, columns].astype(jnp.float32).reshape(rows, width)
    gate = spread(gate_ref[:, columns])
    frozen = times(2 * rows, frozen_refs)
    trainee = times(rows, trainee_refs)
    for k, branch in enumerate((frozen[:rows], frozen[rows:], trainee)):
        mixed = states + gate * branch
        mixed_s[k, :, columns] = mixed
        square = mixed * mixed
        total = square[:, :128]
        for c in range(1, width // 128):
            total = total + square[:, c * 128:(c + 1) * 128]
        square_s[k] += total

    @pl.when(step == pl.num_programs(0) - 1)
    def _():
        lift = 1.0 + spread(scale_ref[...])
        velocities = []
        for k in range(3):
            mean = jnp.sum(square_s[k], axis=1, keepdims=True) * (1.0 / WIDTH)
            root = lax.rsqrt(mean + 1e-06)
            normed = (mixed_s[k] * root * lift).astype(jnp.bfloat16)
            velocities.append(jnp.dot(normed, head_ref[...], preferred_element_type=jnp.float32))
        velocity_c, velocity_n, velocity_s = velocities
        target = velocity_n - (velocity_c - velocity_n)
        pull = (velocity_s - target) * (2.0 / SAMPLES)
        high = pull.astype(jnp.bfloat16)
        low = (pull - high.astype(jnp.float32)).astype(jnp.bfloat16)
        contract = (((1,), (1,)), ((), ()))
        inner = lax.dot_general(high, head_ref[...], contract, preferred_element_type=jnp.float32)
        inner += lax.dot_general(low, head_ref[...], contract, preferred_element_type=jnp.float32)
        inner = inner * lift
        mixed = mixed_s[2]
        along = jnp.sum(inner * mixed, axis=1, keepdims=True) * (1.0 / WIDTH)
        cot = root * inner - mixed * (root * root * root * along)
        cot_ref[...] = (cot * spread(gate_ref[...])).astype(cot_ref.dtype)


def project(back, heads, weights, states, gate, scale, final_head):
    samples, image_dev = states.shape[:2]
    rows = samples * image_dev
    inner = HEADS * HEAD_DIM
    width = 256
    steps = WIDTH // width
    whole = lambda shape: pl.BlockSpec(shape, lambda n, heads: (0,) * len(shape))
    pieces = len(weights)

    def block_of(piece):
        x, first = piece
        return pl.BlockSpec((x.shape[0], width), lambda n, heads: (0, n + first // width))

    return pl.pallas_call(
        functools.partial(head_kernel, samples, image_dev, pieces),
        grid_spec=pltpu.PrefetchScalarGridSpec(
            num_scalar_prefetch=1,
            grid=(steps,),
            in_specs=[
                whole(back.shape),
                whole(states.shape),
                whole(gate.shape),
                whole(scale.shape),
                whole(final_head.shape),
                *[block_of(frozen) for frozen, _ in weights],
                *[block_of(trainee) for _, trainee in weights],
            ],
            out_specs=[whole((rows, WIDTH)), whole((HEADS, rows, HEAD_DIM))],
            scratch_shapes=[
                pltpu.VMEM((2 * rows, inner), jnp.bfloat16),
                pltpu.VMEM((3, rows, WIDTH), jnp.float32),
                pltpu.VMEM((3, rows, 128), jnp.float32),
            ],
        ),
        out_shape=[
            jax.ShapeDtypeStruct((rows, WIDTH), jnp.bfloat16),
            jax.ShapeDtypeStruct((HEADS, rows, HEAD_DIM), jnp.bfloat16),
        ],
        compiler_params=pltpu.CompilerParams(dimension_semantics=("arbitrary",), vmem_limit_bytes=60 << 20),
        cost_estimate=pl.CostEstimate(
            flops=6 * rows * inner * WIDTH,
            bytes_accessed=4 * inner * WIDTH + 4 * rows * inner,
            transcendentals=3 * rows,
        ),
        name="project",
    )(heads, back, states, gate, scale, final_head, *[x for (x, _), _ in weights],
      *[x for _, (x, _) in weights])


class RowGather:
    def __init__(self, block, group_size):
        self.group_size = group_size
        self.own = block

    def swap(self, x, k):
        return lax.ppermute(x, "seq", [(s, s ^ (1 << k)) for s in range(self.group_size)])

    def near(self, value):
        line, pair = self.swap(self.own, 2), self.swap(self.own, 1)
        value, self.own, line, pair = lax.optimization_barrier((value, self.own, line, pair))
        self.blocks = {0: self.own, 4: line, 2: pair, 6: self.swap(line, 1), 8: self.swap(self.own, 3)}
        return value

    def far(self, value):
        value, self.blocks = lax.optimization_barrier((value, self.blocks))
        line, pair = self.swap(self.blocks[8], 2), self.swap(self.blocks[8], 1)
        self.blocks |= {12: line, 10: pair}
        self.corner = (self.swap(line[:, :WIDTH], 1), self.swap(pair[:, WIDTH:], 2))
        return value

    def rows(self, position):
        pieces = {n: ((x, 0), (x, WIDTH)) for n, x in self.blocks.items()}
        pieces[14] = tuple((x, 0) for x in self.corner)
        for offset, x in list(self.blocks.items()):
            other = self.swap(x, 0)
            pieces[offset + 1] = ((other, 0), (other, WIDTH))
        pieces[15] = tuple((self.swap(x, 0), 0) for x in self.corner)
        offsets = jnp.array(list(pieces), jnp.int32)
        return list(pieces.values()), (position ^ offsets).astype(jnp.int32)


def product_kernel(first, mine, peer, att_ref, att_peer_ref, cot_ref, cot_peer_ref, *out_refs):
    slots, _, width = out_refs[0].shape
    for part, out_ref in enumerate(out_refs):
        picked = range(part * slots, (part + 1) * slots)
        own = jnp.concatenate([att_ref[mine[i]] for i in picked], axis=1)
        other = jnp.concatenate([att_peer_ref[peer[i]] for i in picked], axis=1)
        start = first + part * (WIDTH // 2)
        columns = slice(start, start + width)
        total = lax.dot_general(
            jnp.concatenate([own, other], axis=0),
            jnp.concatenate([cot_ref[:, columns], cot_peer_ref[:, columns]], axis=0),
            (((0,), (0,)), ((), ())),
            preferred_element_type=jnp.float32,
        )
        out_ref[...] = total.reshape(out_ref.shape).astype(out_ref.dtype)


def product(first, width, blocks, core, att, att_peer, cot, cot_peer):
    slots = blocks.shape[0] // 2
    rows = cot.shape[0]
    out = jax.ShapeDtypeStruct((slots, HEAD_DIM, width), jnp.bfloat16)
    return pl.pallas_call(
        functools.partial(product_kernel, first),
        in_specs=[pl.BlockSpec(memory_space=pltpu.SMEM)] * 2 + [pl.BlockSpec()] * 4,
        out_specs=[pl.BlockSpec()] * 2,
        out_shape=[out, out],
        compiler_params=pltpu.CompilerParams(vmem_limit_bytes=VMEM_PRODUCT),
        cost_estimate=pl.CostEstimate(
            flops=8 * slots * rows * HEAD_DIM * width,
            bytes_accessed=4 * rows * (WIDTH + 2 * slots * HEAD_DIM) + 4 * slots * HEAD_DIM * width,
            transcendentals=0,
        ),
        name="product",
    )(2 * blocks + core, blocks, att, att_peer, cot, cot_peer)


def reduce_by_halving(att, cot, position, group_size):
    levels = group_size.bit_length() - 1
    chips = group_size // 2
    width = WIDTH // 2 // WAVES
    bit = [(position >> k) & 1 for k in range(levels)]

    def swap(x, k):
        return lax.ppermute(x, "seq", [(s, s ^ (1 << k)) for s in range(group_size)])

    by_core = att.reshape(chips, 2, *att.shape[1:])
    cot_peer = swap(cot, 0)
    att_peer = swap(lax.dynamic_index_in_dim(by_core, 1 - bit[0], 1, keepdims=False), 0)
    orders = (tuple(range(1, levels)), tuple(range(2, levels)) + (1,))

    def chip_blocks(keep):
        tables = []
        for order in orders:
            k = order[0] - 1
            ids = [m for m in range(chips) if not (m >> k) & 1]
            wanted = bit[order[0]] if keep else 1 - bit[order[0]]
            tables.append(jnp.array(ids, jnp.int32) + (wanted << k))
        return jnp.concatenate(tables)

    factors = (bit[0], att, att_peer, cot, cot_peer)
    state = {}
    arrived = {}
    for wave in range(WAVES):
        sent = product(wave * width, width, chip_blocks(False), *factors)
        for part, order in enumerate(orders):
            arrived[wave, part] = swap(sent[part], order[0])
    for wave in range(WAVES):
        kept = product(wave * width, width, chip_blocks(True), *factors)
        for part, order in enumerate(orders):
            left = sorted(order[1:], reverse=True)
            shape = (2,) * len(left) + (HEAD_DIM, width)
            state[wave, part] = (kept[part].reshape(shape), arrived[wave, part].reshape(shape), left)
    for level in range(1, levels - 1):
        for wave in range(WAVES):
            for part, order in enumerate(orders):
                keep, got, left = state[wave, part]
                k = order[level]
                axis = left.index(k)

                def half(x, which):
                    return lax.dynamic_index_in_dim(x, which, axis, keepdims=False).astype(jnp.float32)

                def joined(which):
                    return (half(keep, which) + half(got, which)).astype(jnp.bfloat16)

                rest = [n for n in left if n != k]
                state[wave, part] = (joined(bit[k]), swap(joined(1 - bit[k]), k), rest)
    total = []
    for part in range(2):
        for wave in range(WAVES):
            keep, got, _ = state[wave, part]
            total.append(keep.astype(jnp.float32) + got.astype(jnp.float32))
    return jnp.concatenate(total, axis=1)


def shards(
    image_qkv,
    text_kv,
    prompt_ids,
    timesteps,
    image_states,
    frozen_out,
    trainee_out,
    time_mod,
    final_head,
):
    group_size = lax.axis_size("seq")
    position = lax.axis_index("seq")
    image_dev = image_qkv.shape[3]
    text_dev = text_kv.shape[4]
    owned = SAMPLES * HEADS // group_size
    image_items = image_qkv.transpose(2, 1, 0, 3, 4).reshape(group_size, owned, 3 * image_dev, HEAD_DIM)
    text_items = text_kv.transpose(3, 2, 0, 1, 4, 5).reshape(group_size, owned, 4 * text_dev, HEAD_DIM)
    sample_of = (position * owned + jnp.arange(owned, dtype=jnp.int32)) % SAMPLES
    live = jnp.take(prompt_ids, sample_of, axis=1).transpose(1, 0, 2)
    live = (live != 0).astype(jnp.int32)
    half_dim = TIME_DIM // 2
    freqs = jnp.exp(-math.log(10000.0) * jnp.arange(half_dim, dtype=jnp.float32) / half_dim)
    angles = timesteps.astype(jnp.float32)[:, None] * freqs[None, :]
    embedding = jnp.concatenate([jnp.cos(angles), jnp.sin(angles)], 1)
    modulation = jnp.dot(embedding, time_mod.astype(jnp.float32), precision=lax.Precision.HIGHEST)
    gate = modulation[:, :WIDTH]
    scale = modulation[:, WIDTH:]
    exchange = functools.partial(lax.all_to_all, axis_name="seq", split_axis=0, concat_axis=0, tiled=True)
    gathered = exchange(jnp.concatenate([text_items, image_items], axis=2))
    block = jnp.concatenate([frozen_out, trainee_out], axis=1)
    rows = RowGather(block, group_size)
    if group_size == HEADS:
        gathered = rows.near(gathered)
    both = attend(gathered, live, image_dev, text_dev)
    if group_size == HEADS:
        both = rows.far(both)
        weights, heads = rows.rows(position)
    else:
        everything = lax.all_gather(block, "seq", axis=0, tiled=True)
        all_rows = [((everything, 0), (everything, WIDTH))]
        weights, heads = all_rows, jnp.arange(HEADS, dtype=jnp.int32)
    back = exchange(both).reshape(HEADS, SAMPLES, 2, image_dev, HEAD_DIM)
    cot, att = project(back, heads, weights, image_states, gate, scale, final_head)
    if group_size == HEADS:
        return reduce_by_halving(att, cot, position, group_size)
    partial = jnp.einsum("hrd,rc->hdc", att, cot, preferred_element_type=jnp.float32)
    partial = partial.reshape(HEADS * HEAD_DIM, WIDTH).astype(jnp.bfloat16)
    return lax.psum_scatter(partial, "seq", scatter_dimension=0, tiled=True).astype(jnp.float32)


def solution(mesh):
    return jax.shard_map(
        shards,
        mesh=mesh,
        in_specs=(
            P(None, "grp", None, "seq", None),
            P(None, None, "grp", None, "seq", None),
            P(None, "grp", None),
            P("grp"),
            P("grp", "seq", None),
            P("seq", None),
            P(("grp", "seq"), None),
            P(),
            P(),
        ),
        out_specs=P(("grp", "seq"), None),
        check_vma=False,
    )
```

```python
import functools
import math

import jax
import jax.numpy as jnp
from jax import lax
from jax.experimental import pallas as pl
from jax.experimental.pallas import tpu as pltpu
from jax.sharding import PartitionSpec as P

SAMPLES = 4
HEADS = 16
HEAD_DIM = 128
WIDTH = 1536
TIME_DIM = 256
WAVES = 2
VMEM_PRODUCT = 60 << 20
LOG2E = math.log2(math.e)


def attention_kernel(image_dev, text_dev, block_rows, x_ref, live_ref, out_ref, q_s, k_s, v_s, tk_s, tv_s):
    sources = x_ref.shape[0]
    image_all = sources * image_dev
    text_all = sources * text_dev
    block = pl.program_id(1)

    @pl.when(block == 0)
    def _():
        def rows(start, count):
            piece = x_ref[:, 0, start:start + count, :].astype(jnp.float32)
            return piece.reshape(sources * count, HEAD_DIM).astype(jnp.bfloat16)

        ones_image = jnp.ones((image_all, HEAD_DIM), jnp.bfloat16)
        ones_text = jnp.ones((text_all, HEAD_DIM), jnp.bfloat16)
        for p in range(2):
            tk_s[p] = rows(2 * p * text_dev, text_dev)
            tv_s[p, :, :HEAD_DIM] = rows((2 * p + 1) * text_dev, text_dev)
            tv_s[p, :, HEAD_DIM:] = ones_text
        base = 4 * text_dev
        q_s[...] = rows(base, image_dev)
        k_s[...] = rows(base + image_dev, image_dev)
        v_s[:, :HEAD_DIM] = rows(base + 2 * image_dev, image_dev)
        v_s[:, HEAD_DIM:] = ones_image

    factor = HEAD_DIM ** (-0.5) * LOG2E
    contract = (((1,), (1,)), ((), ()))
    start = pl.multiple_of(block * block_rows, 16)
    queries = q_s[pl.ds(start, block_rows), :]
    scores = lax.dot_general(queries, k_s[...], contract, preferred_element_type=jnp.float32)
    image_max = jnp.max(scores, axis=1, keepdims=True) * factor
    weights = jnp.exp2(scores * factor - image_max).astype(jnp.bfloat16)
    image_out = jnp.dot(weights, v_s[...], preferred_element_type=jnp.float32)
    for p in range(2):
        text = lax.dot_general(queries, tk_s[p], contract, preferred_element_type=jnp.float32)
        text = jnp.where(live_ref[0, p:p + 1, :] != 0, text * factor, -jnp.inf)
        pass_max = jnp.maximum(image_max, jnp.max(text, axis=1, keepdims=True))
        ratio = jnp.exp2(image_max - pass_max)
        text_weights = jnp.exp2(text - pass_max).astype(jnp.bfloat16)
        both = ratio * image_out + jnp.dot(text_weights, tv_s[p], preferred_element_type=jnp.float32)
        result = both[:, :HEAD_DIM] / both[:, HEAD_DIM:]
        out_ref[:, 0, p] = result.reshape(block_rows // image_dev, image_dev, HEAD_DIM).astype(out_ref.dtype)


def attend(gathered, live, image_dev, text_dev):
    sources, owned = gathered.shape[:2]
    rows = gathered.shape[2]
    image_all, text_all = sources * image_dev, sources * text_dev
    per_block = 4
    blocks = sources // per_block
    block_rows = per_block * image_dev
    scores_flops = 2 * image_all * (image_all + 2 * text_all) * HEAD_DIM
    return pl.pallas_call(
        functools.partial(attention_kernel, image_dev, text_dev, block_rows),
        grid=(owned, blocks),
        in_specs=[
            pl.BlockSpec((sources, 1, rows, HEAD_DIM), lambda j, i: (0, j, 0, 0)),
            pl.BlockSpec((1, 2, text_all), lambda j, i: (j, 0, 0)),
        ],
        out_specs=pl.BlockSpec((per_block, 1, 2, image_dev, HEAD_DIM), lambda j, i: (i, j, 0, 0, 0)),
        out_shape=jax.ShapeDtypeStruct((sources, owned, 2, image_dev, HEAD_DIM), jnp.bfloat16),
        scratch_shapes=[
            pltpu.VMEM((image_all, HEAD_DIM), jnp.bfloat16),
            pltpu.VMEM((image_all, HEAD_DIM), jnp.bfloat16),
            pltpu.VMEM((image_all, 2 * HEAD_DIM), jnp.bfloat16),
            pltpu.VMEM((2, text_all, HEAD_DIM), jnp.bfloat16),
            pltpu.VMEM((2, text_all, 2 * HEAD_DIM), jnp.bfloat16),
        ],
        compiler_params=pltpu.CompilerParams(
            dimension_semantics=("arbitrary", "arbitrary"), vmem_limit_bytes=48 << 20
        ),
        cost_estimate=pl.CostEstimate(
            flops=2 * owned * scores_flops,
            bytes_accessed=2 * gathered.size + 4 * owned * image_all * HEAD_DIM,
            transcendentals=owned * image_all * (image_all + 2 * text_all),
        ),
        name="attention",
    )(gathered, live)


def head_kernel(
    samples, image_dev, pieces, heads, back_ref, states_ref, gate_ref, scale_ref, head_ref, *refs,
):
    frozen_refs, trainee_refs = refs[:pieces], refs[pieces:2 * pieces]
    cot_ref, att_ref, both_s, mixed_s, square_s = refs[2 * pieces:]
    step = pl.program_id(0)
    rows = samples * image_dev
    width = frozen_refs[0].shape[1]

    @pl.when(step == 0)
    def _():
        for k in range(HEADS):
            h = heads[k]
            for p in range(2):
                piece = back_ref[h, :, p].astype(jnp.float32).reshape(rows, HEAD_DIM).astype(jnp.bfloat16)
                both_s[p * rows:(p + 1) * rows, k * HEAD_DIM:(k + 1) * HEAD_DIM] = piece
        square_s[...] = jnp.zeros_like(square_s)

    def spread(values):
        return jnp.concatenate(
            [jnp.broadcast_to(values[b:b + 1, :], (image_dev, values.shape[1])) for b in range(samples)], axis=0
        )

    def times(count, weight_refs):
        weights = jnp.concatenate([weight_ref[...] for weight_ref in weight_refs], axis=0)
        return jnp.dot(both_s[:count, :], weights, preferred_element_type=jnp.float32)

    share = -(-HEADS // (WIDTH // width))
    for i in range(share):
        k = jnp.minimum(step * share + i, HEADS - 1)
        piece = both_s[:rows, pl.ds(pl.multiple_of(k * HEAD_DIM, HEAD_DIM), HEAD_DIM)]
        att_ref[heads[k]] = piece.T
    columns = pl.ds(pl.multiple_of(step * width, 128), width)
    states = states_ref[:, :, columns].astype(jnp.float32).reshape(rows, width)
    gate = spread(gate_ref[:, columns])
    frozen = times(2 * rows, frozen_refs)
    trainee = times(rows, trainee_refs)
    for k, branch in enumerate((frozen[:rows], frozen[rows:], trainee)):
        mixed = states + gate * branch
        mixed_s[k, :, columns] = mixed
        square = mixed * mixed
        total = square[:, :128]
        for c in range(1, width // 128):
            total = total + square[:, c * 128:(c + 1) * 128]
        square_s[k] += total

    @pl.when(step == pl.num_programs(0) - 1)
    def _():
        lift = 1.0 + spread(scale_ref[...])
        velocities = []
        for k in range(3):
            mean = jnp.sum(square_s[k], axis=1, keepdims=True) * (1.0 / WIDTH)
            root = lax.rsqrt(mean + 1e-06)
            normed = (mixed_s[k] * root * lift).astype(jnp.bfloat16)
            velocities.append(jnp.dot(normed, head_ref[...], preferred_element_type=jnp.float32))
        velocity_c, velocity_n, velocity_s = velocities
        target = velocity_n - (velocity_c - velocity_n)
        pull = (velocity_s - target) * (2.0 / SAMPLES)
        high = pull.astype(jnp.bfloat16)
        low = (pull - high.astype(jnp.float32)).astype(jnp.bfloat16)
        contract = (((1,), (1,)), ((), ()))
        inner = lax.dot_general(high, head_ref[...], contract, preferred_element_type=jnp.float32)
        inner += lax.dot_general(low, head_ref[...], contract, preferred_element_type=jnp.float32)
        inner = inner * lift
        mixed = mixed_s[2]
        along = jnp.sum(inner * mixed, axis=1, keepdims=True) * (1.0 / WIDTH)
        cot = root * inner - mixed * (root * root * root * along)
        cot_ref[...] = (cot * spread(gate_ref[...])).astype(cot_ref.dtype)


def project(back, heads, weights, states, gate, scale, final_head):
    samples, image_dev = states.shape[:2]
    rows = samples * image_dev
    inner = HEADS * HEAD_DIM
    width = 256
    steps = WIDTH // width
    whole = lambda shape: pl.BlockSpec(shape, lambda n, heads: (0,) * len(shape))
    pieces = len(weights)

    def block_of(piece):
        x, first = piece
        return pl.BlockSpec((x.shape[0], width), lambda n, heads: (0, n + first // width))

    return pl.pallas_call(
        functools.partial(head_kernel, samples, image_dev, pieces),
        grid_spec=pltpu.PrefetchScalarGridSpec(
            num_scalar_prefetch=1,
            grid=(steps,),
            in_specs=[
                whole(back.shape),
                whole(states.shape),
                whole(gate.shape),
                whole(scale.shape),
                whole(final_head.shape),
                *[block_of(frozen) for frozen, _ in weights],
                *[block_of(trainee) for _, trainee in weights],
            ],
            out_specs=[whole((rows, WIDTH)), whole((HEADS, HEAD_DIM, rows))],
            scratch_shapes=[
                pltpu.VMEM((2 * rows, inner), jnp.bfloat16),
                pltpu.VMEM((3, rows, WIDTH), jnp.float32),
                pltpu.VMEM((3, rows, 128), jnp.float32),
            ],
        ),
        out_shape=[
            jax.ShapeDtypeStruct((rows, WIDTH), jnp.bfloat16),
            jax.ShapeDtypeStruct((HEADS, HEAD_DIM, rows), jnp.bfloat16),
        ],
        compiler_params=pltpu.CompilerParams(dimension_semantics=("arbitrary",), vmem_limit_bytes=60 << 20),
        cost_estimate=pl.CostEstimate(
            flops=6 * rows * inner * WIDTH,
            bytes_accessed=4 * inner * WIDTH + 4 * rows * inner,
            transcendentals=3 * rows,
        ),
        name="project",
    )(heads, back, states, gate, scale, final_head, *[x for (x, _), _ in weights],
      *[x for _, (x, _) in weights])


class RowGather:
    def __init__(self, frozen, trainee, group_size):
        self.group_size = group_size
        self.parts = (frozen, trainee)
        self.own = jnp.concatenate([frozen, trainee], axis=1)

    def swap(self, x, k):
        return lax.ppermute(x, "seq", [(s, s ^ (1 << k)) for s in range(self.group_size)])

    def near(self, value):
        line, pair = self.swap(self.own, 2), self.swap(self.own, 1)
        value, self.own, self.parts, line, pair = lax.optimization_barrier(
            (value, self.own, self.parts, line, pair)
        )
        self.blocks = {0: self.own, 4: line, 2: pair, 6: self.swap(line, 1)}
        self.across = [self.swap(x, 3) for x in self.parts]
        return value

    def far(self, value):
        value, self.across[0] = lax.optimization_barrier((value, self.across[0]))
        line, pair = [self.swap(self.across[0], k) for k in (2, 1)]
        value, self.blocks, self.across, line, pair = lax.optimization_barrier(
            (value, self.blocks, self.across, line, pair)
        )
        corner = self.swap(line, 1)
        line_t, pair_t = [self.swap(self.across[1], k) for k in (2, 1)]
        self.split = {8: tuple(self.across), 12: (line, line_t), 10: (pair, pair_t),
                      14: (corner, self.swap(pair_t, 2))}
        return value

    def rows(self, position):
        pieces = {n: ((x, 0), (x, WIDTH)) for n, x in self.blocks.items()}
        pieces |= {n: tuple((x, 0) for x in pair) for n, pair in self.split.items()}
        for offset, x in self.blocks.items():
            other = self.swap(x, 0)
            pieces[offset + 1] = ((other, 0), (other, WIDTH))
        for offset, pair in self.split.items():
            pieces[offset + 1] = tuple((self.swap(x, 0), 0) for x in pair)
        offsets = jnp.array(list(pieces), jnp.int32)
        return list(pieces.values()), (position ^ offsets).astype(jnp.int32)


def product_kernel(starts, mine, peer, att_ref, att_peer_ref, cot_ref, cot_peer_ref, *out_refs):
    slots, _, width = out_refs[0].shape
    for part in range(2):
        picked = range(part * slots, (part + 1) * slots)
        own = jnp.concatenate([att_ref[mine[i]] for i in picked], axis=0)
        other = jnp.concatenate([att_peer_ref[peer[i]] for i in picked], axis=0)
        for start, out_ref in zip(starts, out_refs[part::2]):
            columns = slice(part * (WIDTH // 2) + start, part * (WIDTH // 2) + start + width)
            total = jnp.dot(own, cot_ref[:, columns], preferred_element_type=jnp.float32)
            total += jnp.dot(other, cot_peer_ref[:, columns], preferred_element_type=jnp.float32)
            out_ref[...] = total.reshape(out_ref.shape).astype(out_ref.dtype)


def product(starts, width, blocks, core, att, att_peer, cot, cot_peer):
    slots = blocks.shape[0] // 2
    rows = cot.shape[0]
    out = jax.ShapeDtypeStruct((slots, HEAD_DIM, width), jnp.bfloat16)
    count = 2 * len(starts)
    return pl.pallas_call(
        functools.partial(product_kernel, starts),
        in_specs=[pl.BlockSpec(memory_space=pltpu.SMEM)] * 2 + [pl.BlockSpec()] * 4,
        out_specs=[pl.BlockSpec()] * count,
        out_shape=[out] * count,
        compiler_params=pltpu.CompilerParams(vmem_limit_bytes=VMEM_PRODUCT),
        cost_estimate=pl.CostEstimate(
            flops=4 * count * slots * rows * HEAD_DIM * width,
            bytes_accessed=4 * rows * (WIDTH + 2 * slots * HEAD_DIM) + 2 * count * slots * HEAD_DIM * width,
            transcendentals=0,
        ),
        name="product",
    )(2 * blocks + core, blocks, att, att_peer, cot, cot_peer)


def reduce_by_halving(att, cot, position, group_size):
    levels = group_size.bit_length() - 1
    chips = group_size // 2
    width = WIDTH // 2 // WAVES
    bit = [(position >> k) & 1 for k in range(levels)]

    def swap(x, k):
        return lax.ppermute(x, "seq", [(s, s ^ (1 << k)) for s in range(group_size)])

    by_core = att.reshape(chips, 2, *att.shape[1:])
    cot_peer = swap(cot, 0)
    att_peer = swap(lax.dynamic_index_in_dim(by_core, 1 - bit[0], 1, keepdims=False), 0)
    orders = (tuple(range(1, levels)), (2, 1) + tuple(range(3, levels)))

    def chip_blocks(keep):
        tables = []
        for order in orders:
            k = order[0] - 1
            ids = [m for m in range(chips) if not (m >> k) & 1]
            wanted = bit[order[0]] if keep else 1 - bit[order[0]]
            tables.append(jnp.array(ids, jnp.int32) + (wanted << k))
        return jnp.concatenate(tables)

    factors = (bit[0], att, att_peer, cot, cot_peer)
    state = {}
    arrived = {}
    waves = tuple(wave * width for wave in range(WAVES))
    sent_all = product(waves, width, chip_blocks(False), *factors)
    for wave in range(WAVES):
        sent = sent_all[2 * wave:2 * wave + 2]
        for part, order in enumerate(orders):
            arrived[wave, part] = swap(sent[part], order[0])
    kept_all = product(waves, width, chip_blocks(True), *factors)
    for wave in range(WAVES):
        kept = kept_all[2 * wave:2 * wave + 2]
        for part, order in enumerate(orders):
            left = sorted(order[1:], reverse=True)
            shape = (2,) * len(left) + (HEAD_DIM, width)
            state[wave, part] = (kept[part].reshape(shape), arrived[wave, part].reshape(shape), left)
    for level in range(1, levels - 1):
        for wave in range(WAVES):
            for part, order in enumerate(orders):
                keep, got, left = state[wave, part]
                k = order[level]
                axis = left.index(k)

                def half(x, which):
                    return lax.dynamic_index_in_dim(x, which, axis, keepdims=False).astype(jnp.float32)

                def joined(which):
                    return (half(keep, which) + half(got, which)).astype(jnp.bfloat16)

                rest = [n for n in left if n != k]
                state[wave, part] = (joined(bit[k]), swap(joined(1 - bit[k]), k), rest)
    total = []
    for part in range(2):
        for wave in range(WAVES):
            keep, got, _ = state[wave, part]
            total.append(keep.astype(jnp.float32) + got.astype(jnp.float32))
    return jnp.concatenate(total, axis=1)


def shards(
    image_qkv,
    text_kv,
    prompt_ids,
    timesteps,
    image_states,
    frozen_out,
    trainee_out,
    time_mod,
    final_head,
):
    group_size = lax.axis_size("seq")
    position = lax.axis_index("seq")
    image_dev = image_qkv.shape[3]
    text_dev = text_kv.shape[4]
    owned = SAMPLES * HEADS // group_size
    image_items = image_qkv.transpose(2, 1, 0, 3, 4).reshape(group_size, owned, 3 * image_dev, HEAD_DIM)
    text_items = text_kv.transpose(3, 2, 0, 1, 4, 5).reshape(group_size, owned, 4 * text_dev, HEAD_DIM)
    sample_of = (position * owned + jnp.arange(owned, dtype=jnp.int32)) % SAMPLES
    live = jnp.take(prompt_ids, sample_of, axis=1).transpose(1, 0, 2)
    live = (live != 0).astype(jnp.int32)
    half_dim = TIME_DIM // 2
    freqs = jnp.exp(-math.log(10000.0) * jnp.arange(half_dim, dtype=jnp.float32) / half_dim)
    angles = timesteps.astype(jnp.float32)[:, None] * freqs[None, :]
    embedding = jnp.concatenate([jnp.cos(angles), jnp.sin(angles)], 1)
    modulation = jnp.dot(embedding, time_mod.astype(jnp.float32), precision=lax.Precision.HIGHEST)
    gate = modulation[:, :WIDTH]
    scale = modulation[:, WIDTH:]
    exchange = functools.partial(lax.all_to_all, axis_name="seq", split_axis=0, concat_axis=0, tiled=True)
    gathered = exchange(jnp.concatenate([text_items, image_items], axis=2))
    if group_size == HEADS:
        rows = RowGather(frozen_out, trainee_out, group_size)
        gathered = rows.near(gathered)
    both = attend(gathered, live, image_dev, text_dev)
    if group_size == HEADS:
        both = rows.far(both)
        weights, heads = rows.rows(position)
    else:
        block = jnp.concatenate([frozen_out, trainee_out], axis=1)
        everything = lax.all_gather(block, "seq", axis=0, tiled=True)
        all_rows = [((everything, 0), (everything, WIDTH))]
        weights, heads = all_rows, jnp.arange(HEADS, dtype=jnp.int32)
    back = exchange(both).reshape(HEADS, SAMPLES, 2, image_dev, HEAD_DIM)
    cot, att = project(back, heads, weights, image_states, gate, scale, final_head)
    if group_size == HEADS:
        return reduce_by_halving(att, cot, position, group_size)
    partial = jnp.einsum("hdr,rc->hdc", att, cot, preferred_element_type=jnp.float32)
    partial = partial.reshape(HEADS * HEAD_DIM, WIDTH).astype(jnp.bfloat16)
    return lax.psum_scatter(partial, "seq", scatter_dimension=0, tiled=True).astype(jnp.float32)


def solution(mesh):
    return jax.shard_map(
        shards,
        mesh=mesh,
        in_specs=(
            P(None, "grp", None, "seq", None),
            P(None, None, "grp", None, "seq", None),
            P(None, "grp", None),
            P("grp"),
            P("grp", "seq", None),
            P("seq", None),
            P(("grp", "seq"), None),
            P(),
            P(),
        ),
        out_specs=P(("grp", "seq"), None),
        check_vma=False,
    )
```

```python
import functools
import math

import jax
import jax.numpy as jnp
from jax import lax
from jax.experimental import pallas as pl
from jax.experimental.pallas import tpu as pltpu
from jax.sharding import PartitionSpec as P

SAMPLES = 4
HEADS = 16
HEAD_DIM = 128
WIDTH = 1536
TIME_DIM = 256
WAVES = 2
VMEM_PRODUCT = 60 << 20
LOG2E = math.log2(math.e)


def attention_kernel(image_dev, text_dev, block_rows, x_ref, live_ref, out_ref, q_s, k_s, v_s, tk_s, tv_s):
    sources = x_ref.shape[0]
    image_all = sources * image_dev
    text_all = sources * text_dev
    block = pl.program_id(1)

    @pl.when(block == 0)
    def _():
        def rows(start, count):
            piece = x_ref[:, 0, start:start + count, :].astype(jnp.float32)
            return piece.reshape(sources * count, HEAD_DIM).astype(jnp.bfloat16)

        ones_image = jnp.ones((image_all, HEAD_DIM), jnp.bfloat16)
        ones_text = jnp.ones((text_all, HEAD_DIM), jnp.bfloat16)
        for p in range(2):
            tk_s[p] = rows(2 * p * text_dev, text_dev)
            tv_s[p, :, :HEAD_DIM] = rows((2 * p + 1) * text_dev, text_dev)
            tv_s[p, :, HEAD_DIM:] = ones_text
        base = 4 * text_dev
        q_s[...] = rows(base, image_dev)
        k_s[...] = rows(base + image_dev, image_dev)
        v_s[:, :HEAD_DIM] = rows(base + 2 * image_dev, image_dev)
        v_s[:, HEAD_DIM:] = ones_image

    factor = HEAD_DIM ** (-0.5) * LOG2E
    contract = (((1,), (1,)), ((), ()))
    start = pl.multiple_of(block * block_rows, 16)
    queries = q_s[pl.ds(start, block_rows), :]
    scores = lax.dot_general(queries, k_s[...], contract, preferred_element_type=jnp.float32)
    image_max = jnp.max(scores, axis=1, keepdims=True) * factor
    weights = jnp.exp2(scores * factor - image_max).astype(jnp.bfloat16)
    image_out = jnp.dot(weights, v_s[...], preferred_element_type=jnp.float32)
    for p in range(2):
        text = lax.dot_general(queries, tk_s[p], contract, preferred_element_type=jnp.float32)
        text = jnp.where(live_ref[0, p:p + 1, :] != 0, text * factor, -jnp.inf)
        pass_max = jnp.maximum(image_max, jnp.max(text, axis=1, keepdims=True))
        ratio = jnp.exp2(image_max - pass_max)
        text_weights = jnp.exp2(text - pass_max).astype(jnp.bfloat16)
        both = ratio * image_out + jnp.dot(text_weights, tv_s[p], preferred_element_type=jnp.float32)
        result = both[:, :HEAD_DIM] / both[:, HEAD_DIM:]
        out_ref[:, 0, p] = result.reshape(block_rows // image_dev, image_dev, HEAD_DIM).astype(out_ref.dtype)


def attend(gathered, live, image_dev, text_dev):
    sources, owned = gathered.shape[:2]
    rows = gathered.shape[2]
    image_all, text_all = sources * image_dev, sources * text_dev
    per_block = 4
    blocks = sources // per_block
    block_rows = per_block * image_dev
    scores_flops = 2 * image_all * (image_all + 2 * text_all) * HEAD_DIM
    return pl.pallas_call(
        functools.partial(attention_kernel, image_dev, text_dev, block_rows),
        grid=(owned, blocks),
        in_specs=[
            pl.BlockSpec((sources, 1, rows, HEAD_DIM), lambda j, i: (0, j, 0, 0)),
            pl.BlockSpec((1, 2, text_all), lambda j, i: (j, 0, 0)),
        ],
        out_specs=pl.BlockSpec((per_block, 1, 2, image_dev, HEAD_DIM), lambda j, i: (i, j, 0, 0, 0)),
        out_shape=jax.ShapeDtypeStruct((sources, owned, 2, image_dev, HEAD_DIM), jnp.bfloat16),
        scratch_shapes=[
            pltpu.VMEM((image_all, HEAD_DIM), jnp.bfloat16),
            pltpu.VMEM((image_all, HEAD_DIM), jnp.bfloat16),
            pltpu.VMEM((image_all, 2 * HEAD_DIM), jnp.bfloat16),
            pltpu.VMEM((2, text_all, HEAD_DIM), jnp.bfloat16),
            pltpu.VMEM((2, text_all, 2 * HEAD_DIM), jnp.bfloat16),
        ],
        compiler_params=pltpu.CompilerParams(
            dimension_semantics=("arbitrary", "arbitrary"), vmem_limit_bytes=48 << 20
        ),
        cost_estimate=pl.CostEstimate(
            flops=2 * owned * scores_flops,
            bytes_accessed=2 * gathered.size + 4 * owned * image_all * HEAD_DIM,
            transcendentals=owned * image_all * (image_all + 2 * text_all),
        ),
        name="attention",
    )(gathered, live)


def head_kernel(
    samples, image_dev, counts, heads, blocks, back_ref, states_ref, gate_ref, scale_ref, head_ref, *refs,
):
    own_refs, other_refs = refs[:counts[0]], refs[counts[0]:counts[0] + counts[1]]
    trainee_refs = refs[counts[0] + counts[1]:sum(counts)]
    cot_ref, att_ref, both_s, mixed_s, square_s = refs[sum(counts):]
    step = pl.program_id(0)
    rows = samples * image_dev
    width = own_refs[0].shape[1]

    @pl.when(step == 0)
    def _():
        for k in range(HEADS):
            h = heads[k]
            for p in range(2):
                piece = back_ref[h, :, p].astype(jnp.float32).reshape(rows, HEAD_DIM).astype(jnp.bfloat16)
                both_s[p * rows:(p + 1) * rows, k * HEAD_DIM:(k + 1) * HEAD_DIM] = piece
        square_s[...] = jnp.zeros_like(square_s)

    def spread(values):
        return jnp.concatenate(
            [jnp.broadcast_to(values[b:b + 1, :], (image_dev, values.shape[1])) for b in range(samples)], axis=0
        )

    def stacked(weight_refs):
        return jnp.concatenate([weight_ref[...] for weight_ref in weight_refs], axis=0)

    share = -(-HEADS // (WIDTH // width))
    for i in range(share):
        k = jnp.minimum(step * share + i, HEADS - 1)
        piece = both_s[:rows, pl.ds(pl.multiple_of(k * HEAD_DIM, HEAD_DIM), HEAD_DIM)]
        att_ref[heads[k]] = piece.T
    columns = pl.ds(pl.multiple_of(blocks[step] * width, 128), width)
    states = states_ref[:, :, columns].astype(jnp.float32).reshape(rows, width)
    gate = spread(gate_ref[:, columns])
    weights = jnp.where(step < pl.num_programs(0) // 2, stacked(own_refs), stacked(other_refs))
    frozen = jnp.dot(both_s[...], weights, preferred_element_type=jnp.float32)
    trainee = jnp.dot(both_s[:rows, :], stacked(trainee_refs), preferred_element_type=jnp.float32)
    for k, branch in enumerate((frozen[:rows], frozen[rows:], trainee)):
        mixed = states + gate * branch
        mixed_s[k, :, columns] = mixed
        square = mixed * mixed
        total = square[:, :128]
        for c in range(1, width // 128):
            total = total + square[:, c * 128:(c + 1) * 128]
        square_s[k] += total

    @pl.when(step == pl.num_programs(0) - 1)
    def _():
        lift = 1.0 + spread(scale_ref[...])
        contract = (((1,), (1,)), ((), ()))
        velocities = []
        for k in range(3):
            mean = jnp.sum(square_s[k], axis=1, keepdims=True) * (1.0 / WIDTH)
            root = lax.rsqrt(mean + 1e-06)
            normed = (mixed_s[k] * root * lift).astype(jnp.bfloat16)
            velocities.append(
                lax.dot_general(normed, head_ref[...], contract, preferred_element_type=jnp.float32)
            )
        velocity_c, velocity_n, velocity_s = velocities
        target = velocity_n - (velocity_c - velocity_n)
        pull = (velocity_s - target) * (2.0 / SAMPLES)
        high = pull.astype(jnp.bfloat16)
        low = (pull - high.astype(jnp.float32)).astype(jnp.bfloat16)
        inner = jnp.dot(high, head_ref[...], preferred_element_type=jnp.float32)
        inner += jnp.dot(low, head_ref[...], preferred_element_type=jnp.float32)
        inner = inner * lift
        mixed = mixed_s[2]
        along = jnp.sum(inner * mixed, axis=1, keepdims=True) * (1.0 / WIDTH)
        cot = root * inner - mixed * (root * root * root * along)
        cot_ref[...] = (cot * spread(gate_ref[...])).astype(cot_ref.dtype)


def project(back, heads, half, weights, states, gate, scale, head_rows):
    samples, image_dev = states.shape[:2]
    rows = samples * image_dev
    inner = HEADS * HEAD_DIM
    width = 256
    steps = WIDTH // width
    blocks = (jnp.arange(steps, dtype=jnp.int32) + half * (steps // 2)) % steps
    whole = lambda shape: pl.BlockSpec(shape, lambda n, heads, blocks: (0,) * len(shape))
    places = (
        lambda n, blocks: jnp.minimum(n, steps // 2 - 1),
        lambda n, blocks: jnp.maximum(n - steps // 2, 0),
        lambda n, blocks: blocks[n],
    )

    def block_of(x, first, place):
        return pl.BlockSpec((x.shape[0], width), lambda n, heads, blocks: (0, place(n, blocks) + first // width))

    return pl.pallas_call(
        functools.partial(head_kernel, samples, image_dev, tuple(len(pieces) for pieces in weights)),
        grid_spec=pltpu.PrefetchScalarGridSpec(
            num_scalar_prefetch=2,
            grid=(steps,),
            in_specs=[
                whole(back.shape),
                whole(states.shape),
                whole(gate.shape),
                whole(scale.shape),
                whole(head_rows.shape),
                *[block_of(x, first, place) for pieces, place in zip(weights, places) for x, first in pieces],
            ],
            out_specs=[whole((rows, WIDTH)), whole((HEADS, HEAD_DIM, rows))],
            scratch_shapes=[
                pltpu.VMEM((2 * rows, inner), jnp.bfloat16),
                pltpu.VMEM((3, rows, WIDTH), jnp.float32),
                pltpu.VMEM((3, rows, 128), jnp.float32),
            ],
        ),
        out_shape=[
            jax.ShapeDtypeStruct((rows, WIDTH), jnp.bfloat16),
            jax.ShapeDtypeStruct((HEADS, HEAD_DIM, rows), jnp.bfloat16),
        ],
        compiler_params=pltpu.CompilerParams(dimension_semantics=("arbitrary",), vmem_limit_bytes=60 << 20),
        cost_estimate=pl.CostEstimate(
            flops=6 * rows * inner * WIDTH,
            bytes_accessed=4 * inner * WIDTH + 4 * rows * inner,
            transcendentals=3 * rows,
        ),
        name="project",
    )(heads, blocks, back, states, gate, scale, head_rows, *[x for pieces in weights for x, _ in pieces])


class RowGather:
    def __init__(self, frozen, trainee, half, group_size, groups):
        self.group_size, self.groups = group_size, groups
        self.cut = WIDTH // 2
        self.own = jnp.concatenate(
            [lax.dynamic_slice_in_dim(frozen, half * self.cut, self.cut, axis=1), trainee], axis=1
        )

    def swap(self, x, k):
        return lax.ppermute(x, "seq", [(s, s ^ (1 << k)) for s in range(self.group_size)])

    def across(self, *blocks):
        halves = jnp.concatenate([x[:, :self.cut] for x in blocks])
        return lax.ppermute(halves, "grp", [(g, g ^ 1) for g in range(self.groups)])

    def near(self, value):
        line, pair = self.swap(self.own, 2), self.swap(self.own, 1)
        value, self.own, line, pair = lax.optimization_barrier((value, self.own, line, pair))
        self.blocks = [self.own, line, pair, self.swap(line, 1), self.swap(self.own, 3)]
        return value

    def far(self, value):
        value, self.blocks = lax.optimization_barrier((value, self.blocks))
        line, pair = self.swap(self.blocks[4], 2), self.swap(self.blocks[4], 1)
        value, line, pair = lax.optimization_barrier((value, line, pair))
        self.corner = (self.swap(line[:, :self.cut], 1), self.swap(pair[:, self.cut:], 2))
        self.others = [self.across(*self.blocks[:4])]
        self.blocks += [line, pair]
        self.others += [self.across(*self.blocks[4:]), self.across(self.corner[0])]
        return value

    def rows(self, position):
        def pieces(blocks, corner, others):
            return (
                [(x, 0) for x in blocks] + [(corner[0], 0)],
                [(x, 0) for x in others],
                [(x, self.cut) for x in blocks] + [(corner[1], 0)],
            )

        mine = pieces(self.blocks, self.corner, self.others)
        core = pieces(*[[self.swap(x, 0) for x in group] for group in (self.blocks, self.corner, self.others)])
        offsets = jnp.array([0, 4, 2, 6, 8, 12, 10, 14], jnp.int32)
        heads = position ^ jnp.concatenate([offsets, offsets + 1])
        return [a + b for a, b in zip(mine, core)], heads.astype(jnp.int32)


def product_kernel(starts, mine, peer, att_ref, att_peer_ref, cot_ref, cot_peer_ref, *out_refs):
    slots, _, width = out_refs[0].shape
    for part in range(2):
        picked = range(part * slots, (part + 1) * slots)
        own = jnp.concatenate([att_ref[mine[i]] for i in picked], axis=0)
        other = jnp.concatenate([att_peer_ref[peer[i]] for i in picked], axis=0)
        for start, out_ref in zip(starts, out_refs[part::2]):
            columns = slice(part * (WIDTH // 2) + start, part * (WIDTH // 2) + start + width)
            total = jnp.dot(own, cot_ref[:, columns], preferred_element_type=jnp.float32)
            total += jnp.dot(other, cot_peer_ref[:, columns], preferred_element_type=jnp.float32)
            out_ref[...] = total.reshape(out_ref.shape).astype(out_ref.dtype)


def product(starts, width, blocks, core, att, att_peer, cot, cot_peer):
    slots = blocks.shape[0] // 2
    rows = cot.shape[0]
    out = jax.ShapeDtypeStruct((slots, HEAD_DIM, width), jnp.bfloat16)
    count = 2 * len(starts)
    return pl.pallas_call(
        functools.partial(product_kernel, starts),
        in_specs=[pl.BlockSpec(memory_space=pltpu.SMEM)] * 2 + [pl.BlockSpec()] * 4,
        out_specs=[pl.BlockSpec()] * count,
        out_shape=[out] * count,
        compiler_params=pltpu.CompilerParams(vmem_limit_bytes=VMEM_PRODUCT),
        cost_estimate=pl.CostEstimate(
            flops=4 * count * slots * rows * HEAD_DIM * width,
            bytes_accessed=4 * rows * (WIDTH + 2 * slots * HEAD_DIM) + 2 * count * slots * HEAD_DIM * width,
            transcendentals=0,
        ),
        name="product",
    )(2 * blocks + core, blocks, att, att_peer, cot, cot_peer)


def reduce_by_halving(att, cot, position, group_size):
    levels = group_size.bit_length() - 1
    chips = group_size // 2
    width = WIDTH // 2 // WAVES
    bit = [(position >> k) & 1 for k in range(levels)]

    def swap(x, k):
        return lax.ppermute(x, "seq", [(s, s ^ (1 << k)) for s in range(group_size)])

    by_core = att.reshape(chips, 2, *att.shape[1:])
    cot_peer = swap(cot, 0)
    att_peer = swap(lax.dynamic_index_in_dim(by_core, 1 - bit[0], 1, keepdims=False), 0)
    orders = (tuple(range(1, levels)), (2, 1) + tuple(range(3, levels)))

    def chip_blocks(keep):
        tables = []
        for order in orders:
            k = order[0] - 1
            ids = [m for m in range(chips) if not (m >> k) & 1]
            wanted = bit[order[0]] if keep else 1 - bit[order[0]]
            tables.append(jnp.array(ids, jnp.int32) + (wanted << k))
        return jnp.concatenate(tables)

    factors = (bit[0], att, att_peer, cot, cot_peer)
    state = {}
    arrived = {}
    waves = tuple(wave * width for wave in range(WAVES))
    sent_all = product(waves, width, chip_blocks(False), *factors)
    for wave in range(WAVES):
        sent = sent_all[2 * wave:2 * wave + 2]
        for part, order in enumerate(orders):
            arrived[wave, part] = swap(sent[part], order[0])
    kept_all = product(waves, width, chip_blocks(True), *factors)
    for wave in range(WAVES):
        kept = kept_all[2 * wave:2 * wave + 2]
        for part, order in enumerate(orders):
            left = sorted(order[1:], reverse=True)
            shape = (2,) * len(left) + (HEAD_DIM, width)
            state[wave, part] = (kept[part].reshape(shape), arrived[wave, part].reshape(shape), left)
    for level in range(1, levels - 1):
        for wave in range(WAVES):
            for part, order in enumerate(orders):
                keep, got, left = state[wave, part]
                k = order[level]
                axis = left.index(k)

                def half(x, which):
                    return lax.dynamic_index_in_dim(x, which, axis, keepdims=False).astype(jnp.float32)

                def joined(which):
                    return (half(keep, which) + half(got, which)).astype(jnp.bfloat16)

                rest = [n for n in left if n != k]
                state[wave, part] = (joined(bit[k]), swap(joined(1 - bit[k]), k), rest)
    total = []
    for part in range(2):
        for wave in range(WAVES):
            keep, got, _ = state[wave, part]
            total.append(keep.astype(jnp.float32) + got.astype(jnp.float32))
    return jnp.concatenate(total, axis=1)


def shards(
    image_qkv,
    text_kv,
    prompt_ids,
    timesteps,
    image_states,
    frozen_out,
    trainee_out,
    time_mod,
    final_head,
):
    group_size = lax.axis_size("seq")
    position = lax.axis_index("seq")
    image_dev = image_qkv.shape[3]
    text_dev = text_kv.shape[4]
    owned = SAMPLES * HEADS // group_size
    image_items = image_qkv.transpose(2, 1, 0, 3, 4).reshape(group_size, owned, 3 * image_dev, HEAD_DIM)
    text_items = text_kv.transpose(3, 2, 0, 1, 4, 5).reshape(group_size, owned, 4 * text_dev, HEAD_DIM)
    sample_of = (position * owned + jnp.arange(owned, dtype=jnp.int32)) % SAMPLES
    live = jnp.take(prompt_ids, sample_of, axis=1).transpose(1, 0, 2)
    live = (live != 0).astype(jnp.int32)
    half_dim = TIME_DIM // 2
    freqs = jnp.exp(-math.log(10000.0) * jnp.arange(half_dim, dtype=jnp.float32) / half_dim)
    angles = timesteps.astype(jnp.float32)[:, None] * freqs[None, :]
    embedding = jnp.concatenate([jnp.cos(angles), jnp.sin(angles)], 1)
    modulation = jnp.dot(embedding, time_mod.astype(jnp.float32), precision=lax.Precision.HIGHEST)
    gate = modulation[:, :WIDTH]
    scale = modulation[:, WIDTH:]
    exchange = functools.partial(lax.all_to_all, axis_name="seq", split_axis=0, concat_axis=0, tiled=True)
    gathered = exchange(jnp.concatenate([text_items, image_items], axis=2))
    groups = lax.axis_size("grp")
    staged = group_size == HEADS and groups % 2 == 0
    gathered, gate, scale = lax.optimization_barrier((gathered, gate, scale))
    if staged:
        half = lax.axis_index("grp") % 2
        rows = RowGather(frozen_out, trainee_out, half, group_size, groups)
        gathered = rows.near(gathered)
    both = attend(gathered, live, image_dev, text_dev)
    if staged:
        both = rows.far(both)
        weights, heads = rows.rows(position)
    else:
        half, heads = jnp.int32(0), jnp.arange(HEADS, dtype=jnp.int32)
        block = jnp.concatenate([frozen_out, trainee_out], axis=1)
        everything = lax.all_gather(block, "seq", axis=0, tiled=True)
        weights = [[(everything, first)] for first in (0, WIDTH // 2, WIDTH)]
    back = exchange(both).reshape(HEADS, SAMPLES, 2, image_dev, HEAD_DIM)
    cot, att = project(back, heads, half, weights, image_states, gate, scale, final_head.T)
    if group_size == HEADS:
        return reduce_by_halving(att, cot, position, group_size)
    partial = jnp.einsum("hdr,rc->hdc", att, cot, preferred_element_type=jnp.float32)
    partial = partial.reshape(HEADS * HEAD_DIM, WIDTH).astype(jnp.bfloat16)
    return lax.psum_scatter(partial, "seq", scatter_dimension=0, tiled=True).astype(jnp.float32)


def solution(mesh):
    return jax.shard_map(
        shards,
        mesh=mesh,
        in_specs=(
            P(None, "grp", None, "seq", None),
            P(None, None, "grp", None, "seq", None),
            P(None, "grp", None),
            P("grp"),
            P("grp", "seq", None),
            P("seq", None),
            P(("grp", "seq"), None),
            P(),
            P(),
        ),
        out_specs=P(("grp", "seq"), None),
        check_vma=False,
    )
```

```python
import functools
import math

import jax
import jax.numpy as jnp
from jax import lax
from jax.experimental import pallas as pl
from jax.experimental.pallas import tpu as pltpu
from jax.sharding import PartitionSpec as P

SAMPLES = 4
HEADS = 16
HEAD_DIM = 128
WIDTH = 1536
TIME_DIM = 256
WAVES = 2
VMEM_PRODUCT = 60 << 20
LOG2E = math.log2(math.e)


def attention_kernel(image_dev, text_dev, block_rows, x_ref, live_ref, out_ref, q_s, k_s, v_s, tk_s, tv_s):
    sources = x_ref.shape[0]
    image_all = sources * image_dev
    text_all = sources * text_dev
    block = pl.program_id(1)

    @pl.when(block == 0)
    def _():
        def rows(start, count):
            piece = x_ref[:, 0, start:start + count, :].astype(jnp.float32)
            return piece.reshape(sources * count, HEAD_DIM).astype(jnp.bfloat16)

        ones_image = jnp.ones((image_all, HEAD_DIM), jnp.bfloat16)
        ones_text = jnp.ones((text_all, HEAD_DIM), jnp.bfloat16)
        for p in range(2):
            tk_s[p] = rows(2 * p * text_dev, text_dev)
            tv_s[p, :, :HEAD_DIM] = rows((2 * p + 1) * text_dev, text_dev)
            tv_s[p, :, HEAD_DIM:] = ones_text
        base = 4 * text_dev
        q_s[...] = rows(base, image_dev)
        k_s[...] = rows(base + image_dev, image_dev)
        v_s[:, :HEAD_DIM] = rows(base + 2 * image_dev, image_dev)
        v_s[:, HEAD_DIM:] = ones_image

    factor = HEAD_DIM ** (-0.5) * LOG2E
    contract = (((1,), (1,)), ((), ()))
    start = pl.multiple_of(block * block_rows, 16)
    queries = q_s[pl.ds(start, block_rows), :]
    scores = lax.dot_general(queries, k_s[...], contract, preferred_element_type=jnp.float32)
    image_max = jnp.max(scores, axis=1, keepdims=True) * factor
    weights = jnp.exp2(scores * factor - image_max).astype(jnp.bfloat16)
    image_out = jnp.dot(weights, v_s[...], preferred_element_type=jnp.float32)
    for p in range(2):
        text = lax.dot_general(queries, tk_s[p], contract, preferred_element_type=jnp.float32)
        text = jnp.where(live_ref[0, p:p + 1, :] != 0, text * factor, -jnp.inf)
        pass_max = jnp.maximum(image_max, jnp.max(text, axis=1, keepdims=True))
        ratio = jnp.exp2(image_max - pass_max)
        text_weights = jnp.exp2(text - pass_max).astype(jnp.bfloat16)
        both = ratio * image_out + jnp.dot(text_weights, tv_s[p], preferred_element_type=jnp.float32)
        result = both[:, :HEAD_DIM] / both[:, HEAD_DIM:]
        out_ref[:, 0, p] = result.reshape(block_rows // image_dev, image_dev, HEAD_DIM).astype(out_ref.dtype)


def attend(gathered, live, image_dev, text_dev):
    sources, owned = gathered.shape[:2]
    rows = gathered.shape[2]
    image_all, text_all = sources * image_dev, sources * text_dev
    per_block = 4
    blocks = sources // per_block
    block_rows = per_block * image_dev
    scores_flops = 2 * image_all * (image_all + 2 * text_all) * HEAD_DIM
    return pl.pallas_call(
        functools.partial(attention_kernel, image_dev, text_dev, block_rows),
        grid=(owned, blocks),
        in_specs=[
            pl.BlockSpec((sources, 1, rows, HEAD_DIM), lambda j, i: (0, j, 0, 0)),
            pl.BlockSpec((1, 2, text_all), lambda j, i: (j, 0, 0)),
        ],
        out_specs=pl.BlockSpec((per_block, 1, 2, image_dev, HEAD_DIM), lambda j, i: (i, j, 0, 0, 0)),
        out_shape=jax.ShapeDtypeStruct((sources, owned, 2, image_dev, HEAD_DIM), jnp.bfloat16),
        scratch_shapes=[
            pltpu.VMEM((image_all, HEAD_DIM), jnp.bfloat16),
            pltpu.VMEM((image_all, HEAD_DIM), jnp.bfloat16),
            pltpu.VMEM((image_all, 2 * HEAD_DIM), jnp.bfloat16),
            pltpu.VMEM((2, text_all, HEAD_DIM), jnp.bfloat16),
            pltpu.VMEM((2, text_all, 2 * HEAD_DIM), jnp.bfloat16),
        ],
        compiler_params=pltpu.CompilerParams(
            dimension_semantics=("arbitrary", "arbitrary"), vmem_limit_bytes=48 << 20
        ),
        cost_estimate=pl.CostEstimate(
            flops=2 * owned * scores_flops,
            bytes_accessed=2 * gathered.size + 4 * owned * image_all * HEAD_DIM,
            transcendentals=owned * image_all * (image_all + 2 * text_all),
        ),
        name="attention",
    )(gathered, live)


def head_kernel(
    samples, image_dev, counts, heads, blocks, back_ref, states_ref, gate_ref, scale_ref, head_ref, *refs,
):
    own_refs, other_refs = refs[:counts[0]], refs[counts[0]:counts[0] + counts[1]]
    trainee_refs = refs[counts[0] + counts[1]:sum(counts)]
    cot_ref, att_ref, both_s, mixed_s, square_s = refs[sum(counts):]
    step = pl.program_id(0)
    rows = samples * image_dev
    width = own_refs[0].shape[1]

    @pl.when(step == 0)
    def _():
        for k in range(HEADS):
            h = heads[k]
            for p in range(2):
                piece = back_ref[h, :, p].astype(jnp.float32).reshape(rows, HEAD_DIM).astype(jnp.bfloat16)
                both_s[p * rows:(p + 1) * rows, k * HEAD_DIM:(k + 1) * HEAD_DIM] = piece
        square_s[...] = jnp.zeros_like(square_s)

    def spread(values):
        return jnp.concatenate(
            [jnp.broadcast_to(values[b:b + 1, :], (image_dev, values.shape[1])) for b in range(samples)], axis=0
        )

    def stacked(weight_refs):
        return jnp.concatenate([weight_ref[...] for weight_ref in weight_refs], axis=0)

    share = -(-HEADS // (WIDTH // width))
    for i in range(share):
        k = jnp.minimum(step * share + i, HEADS - 1)
        piece = both_s[:rows, pl.ds(pl.multiple_of(k * HEAD_DIM, HEAD_DIM), HEAD_DIM)]
        att_ref[heads[k]] = piece.T
    columns = pl.ds(pl.multiple_of(blocks[step] * width, 128), width)
    states = states_ref[:, :, columns].astype(jnp.float32).reshape(rows, width)
    gate = spread(gate_ref[:, columns])
    weights = jnp.where(step < pl.num_programs(0) // 2, stacked(own_refs), stacked(other_refs))
    frozen = jnp.dot(both_s[...], weights, preferred_element_type=jnp.float32)
    trainee = jnp.dot(both_s[:rows, :], stacked(trainee_refs), preferred_element_type=jnp.float32)
    for k, branch in enumerate((frozen[:rows], frozen[rows:], trainee)):
        mixed = states + gate * branch
        mixed_s[k, :, columns] = mixed
        square = mixed * mixed
        total = square[:, :128]
        for c in range(1, width // 128):
            total = total + square[:, c * 128:(c + 1) * 128]
        square_s[k] += total

    @pl.when(step == pl.num_programs(0) - 1)
    def _():
        lift = 1.0 + spread(scale_ref[...])
        contract = (((1,), (1,)), ((), ()))
        velocities = []
        for k in range(3):
            mean = jnp.sum(square_s[k], axis=1, keepdims=True) * (1.0 / WIDTH)
            root = lax.rsqrt(mean + 1e-06)
            normed = (mixed_s[k] * root * lift).astype(jnp.bfloat16)
            velocities.append(
                lax.dot_general(normed, head_ref[...], contract, preferred_element_type=jnp.float32)
            )
        velocity_c, velocity_n, velocity_s = velocities
        target = velocity_n - (velocity_c - velocity_n)
        pull = (velocity_s - target) * (2.0 / SAMPLES)
        high = pull.astype(jnp.bfloat16)
        low = (pull - high.astype(jnp.float32)).astype(jnp.bfloat16)
        inner = jnp.dot(high, head_ref[...], preferred_element_type=jnp.float32)
        inner += jnp.dot(low, head_ref[...], preferred_element_type=jnp.float32)
        inner = inner * lift
        mixed = mixed_s[2]
        along = jnp.sum(inner * mixed, axis=1, keepdims=True) * (1.0 / WIDTH)
        cot = root * inner - mixed * (root * root * root * along)
        cot_ref[...] = (cot * spread(gate_ref[...])).astype(cot_ref.dtype)


def project(back, heads, half, weights, states, gate, scale, head_rows):
    samples, image_dev = states.shape[:2]
    rows = samples * image_dev
    inner = HEADS * HEAD_DIM
    width = 256
    steps = WIDTH // width
    blocks = (jnp.arange(steps, dtype=jnp.int32) + half * (steps // 2)) % steps
    whole = lambda shape: pl.BlockSpec(shape, lambda n, heads, blocks: (0,) * len(shape))
    places = (
        lambda n, blocks: jnp.minimum(n, steps // 2 - 1),
        lambda n, blocks: jnp.maximum(n - steps // 2, 0),
        lambda n, blocks: blocks[n],
    )

    def block_of(x, first, place):
        return pl.BlockSpec((x.shape[0], width), lambda n, heads, blocks: (0, place(n, blocks) + first // width))

    return pl.pallas_call(
        functools.partial(head_kernel, samples, image_dev, tuple(len(pieces) for pieces in weights)),
        grid_spec=pltpu.PrefetchScalarGridSpec(
            num_scalar_prefetch=2,
            grid=(steps,),
            in_specs=[
                whole(back.shape),
                whole(states.shape),
                whole(gate.shape),
                whole(scale.shape),
                whole(head_rows.shape),
                *[block_of(x, first, place) for pieces, place in zip(weights, places) for x, first in pieces],
            ],
            out_specs=[whole((rows, WIDTH)), whole((HEADS, HEAD_DIM, rows))],
            scratch_shapes=[
                pltpu.VMEM((2 * rows, inner), jnp.bfloat16),
                pltpu.VMEM((3, rows, WIDTH), jnp.float32),
                pltpu.VMEM((3, rows, 128), jnp.float32),
            ],
        ),
        out_shape=[
            jax.ShapeDtypeStruct((rows, WIDTH), jnp.bfloat16),
            jax.ShapeDtypeStruct((HEADS, HEAD_DIM, rows), jnp.bfloat16),
        ],
        compiler_params=pltpu.CompilerParams(dimension_semantics=("arbitrary",), vmem_limit_bytes=60 << 20),
        cost_estimate=pl.CostEstimate(
            flops=6 * rows * inner * WIDTH,
            bytes_accessed=4 * inner * WIDTH + 4 * rows * inner,
            transcendentals=3 * rows,
        ),
        name="project",
    )(heads, blocks, back, states, gate, scale, head_rows, *[x for pieces in weights for x, _ in pieces])


class RowGather:
    def __init__(self, frozen, trainee, half, group_size, groups):
        self.group_size, self.groups = group_size, groups
        self.cut = WIDTH // 2
        self.own = jnp.concatenate(
            [lax.dynamic_slice_in_dim(frozen, half * self.cut, self.cut, axis=1), trainee], axis=1
        )

    def swap(self, x, k):
        return lax.ppermute(x, "seq", [(s, s ^ (1 << k)) for s in range(self.group_size)])

    def across(self, *blocks):
        halves = jnp.concatenate([x[:, :self.cut] for x in blocks])
        return lax.ppermute(halves, "grp", [(g, g ^ 1) for g in range(self.groups)])

    def near(self, value):
        line, pair = self.swap(self.own, 2), self.swap(self.own, 1)
        value, self.own, line, pair = lax.optimization_barrier((value, self.own, line, pair))
        self.blocks = [self.own, line, pair, self.swap(line, 1), self.swap(self.own, 3)]
        self.others = [self.across(self.own, line, pair)]
        return value

    def far(self, value):
        value, self.blocks, self.others = lax.optimization_barrier((value, self.blocks, self.others))
        line, pair = self.swap(self.blocks[4], 2), self.swap(self.blocks[4], 1)
        value, line, pair = lax.optimization_barrier((value, line, pair))
        self.corner = (
            self.swap(line[:, :self.cut], 1),
            self.swap(line[:, self.cut:], 1),
        )
        self.blocks += [line, pair]
        self.others += [self.across(*self.blocks[3:]), self.across(self.corner[0])]
        return value

    def rows(self, position):
        def pieces(blocks, corner, others):
            return (
                [(x, 0) for x in blocks] + [(corner[0], 0)],
                [(x, 0) for x in others],
                [(x, self.cut) for x in blocks] + [(corner[1], 0)],
            )

        mine = pieces(self.blocks, self.corner, self.others)
        core = pieces(*[[self.swap(x, 0) for x in group] for group in (self.blocks, self.corner, self.others)])
        offsets = jnp.array([0, 4, 2, 6, 8, 12, 10, 14], jnp.int32)
        heads = position ^ jnp.concatenate([offsets, offsets + 1])
        return [a + b for a, b in zip(mine, core)], heads.astype(jnp.int32)


def product_kernel(starts, mine, peer, att_ref, att_peer_ref, cot_ref, cot_peer_ref, *out_refs):
    slots, _, width = out_refs[0].shape
    for part in range(2):
        picked = range(part * slots, (part + 1) * slots)
        own = jnp.concatenate([att_ref[mine[i]] for i in picked], axis=0)
        other = jnp.concatenate([att_peer_ref[peer[i]] for i in picked], axis=0)
        for start, out_ref in zip(starts, out_refs[part::2]):
            columns = slice(part * (WIDTH // 2) + start, part * (WIDTH // 2) + start + width)
            total = jnp.dot(own, cot_ref[:, columns], preferred_element_type=jnp.float32)
            total += jnp.dot(other, cot_peer_ref[:, columns], preferred_element_type=jnp.float32)
            out_ref[...] = total.reshape(out_ref.shape).astype(out_ref.dtype)


def product(starts, width, blocks, core, att, att_peer, cot, cot_peer):
    slots = blocks.shape[0] // 2
    rows = cot.shape[0]
    out = jax.ShapeDtypeStruct((slots, HEAD_DIM, width), jnp.bfloat16)
    count = 2 * len(starts)
    return pl.pallas_call(
        functools.partial(product_kernel, starts),
        in_specs=[pl.BlockSpec(memory_space=pltpu.SMEM)] * 2 + [pl.BlockSpec()] * 4,
        out_specs=[pl.BlockSpec()] * count,
        out_shape=[out] * count,
        compiler_params=pltpu.CompilerParams(vmem_limit_bytes=VMEM_PRODUCT),
        cost_estimate=pl.CostEstimate(
            flops=4 * count * slots * rows * HEAD_DIM * width,
            bytes_accessed=4 * rows * (WIDTH + 2 * slots * HEAD_DIM) + 2 * count * slots * HEAD_DIM * width,
            transcendentals=0,
        ),
        name="product",
    )(2 * blocks + core, blocks, att, att_peer, cot, cot_peer)


def reduce_by_halving(att, cot, position, group_size):
    levels = group_size.bit_length() - 1
    chips = group_size // 2
    width = WIDTH // 2 // WAVES
    bit = [(position >> k) & 1 for k in range(levels)]

    def swap(x, k):
        return lax.ppermute(x, "seq", [(s, s ^ (1 << k)) for s in range(group_size)])

    by_core = att.reshape(chips, 2, *att.shape[1:])
    cot_peer = swap(cot, 0)
    att_peer = swap(lax.dynamic_index_in_dim(by_core, 1 - bit[0], 1, keepdims=False), 0)
    orders = (tuple(range(1, levels)), (2, 1) + tuple(range(3, levels)))

    def chip_blocks(keep):
        tables = []
        for order in orders:
            k = order[0] - 1
            ids = [m for m in range(chips) if not (m >> k) & 1]
            wanted = bit[order[0]] if keep else 1 - bit[order[0]]
            tables.append(jnp.array(ids, jnp.int32) + (wanted << k))
        return jnp.concatenate(tables)

    factors = (bit[0], att, att_peer, cot, cot_peer)
    state = {}
    arrived = {}
    waves = tuple(wave * width for wave in range(WAVES))
    sent_all = product(waves, width, chip_blocks(False), *factors)
    for wave in range(WAVES):
        sent = sent_all[2 * wave:2 * wave + 2]
        for part, order in enumerate(orders):
            arrived[wave, part] = swap(sent[part], order[0])
    kept_all = product(waves, width, chip_blocks(True), *factors)
    for wave in range(WAVES):
        kept = kept_all[2 * wave:2 * wave + 2]
        for part, order in enumerate(orders):
            left = sorted(order[1:], reverse=True)
            shape = (2,) * len(left) + (HEAD_DIM, width)
            state[wave, part] = (kept[part].reshape(shape), arrived[wave, part].reshape(shape), left)
    for level in range(1, levels - 1):
        for wave in range(WAVES):
            for part, order in enumerate(orders):
                keep, got, left = state[wave, part]
                k = order[level]
                axis = left.index(k)

                def half(x, which):
                    return lax.dynamic_index_in_dim(x, which, axis, keepdims=False).astype(jnp.float32)

                def joined(which):
                    return (half(keep, which) + half(got, which)).astype(jnp.bfloat16)

                rest = [n for n in left if n != k]
                state[wave, part] = (joined(bit[k]), swap(joined(1 - bit[k]), k), rest)
    total = []
    for part in range(2):
        for wave in range(WAVES):
            keep, got, _ = state[wave, part]
            total.append(keep.astype(jnp.float32) + got.astype(jnp.float32))
    return jnp.concatenate(total, axis=1)


def shards(
    image_qkv,
    text_kv,
    prompt_ids,
    timesteps,
    image_states,
    frozen_out,
    trainee_out,
    time_mod,
    final_head,
):
    group_size = lax.axis_size("seq")
    position = lax.axis_index("seq")
    image_dev = image_qkv.shape[3]
    text_dev = text_kv.shape[4]
    owned = SAMPLES * HEADS // group_size
    image_items = image_qkv.transpose(2, 1, 0, 3, 4).reshape(group_size, owned, 3 * image_dev, HEAD_DIM)
    text_items = text_kv.transpose(3, 2, 0, 1, 4, 5).reshape(group_size, owned, 4 * text_dev, HEAD_DIM)
    sample_of = (position * owned + jnp.arange(owned, dtype=jnp.int32)) % SAMPLES
    live = jnp.take(prompt_ids, sample_of, axis=1).transpose(1, 0, 2)
    live = (live != 0).astype(jnp.int32)
    half_dim = TIME_DIM // 2
    freqs = jnp.exp(-math.log(10000.0) * jnp.arange(half_dim, dtype=jnp.float32) / half_dim)
    angles = timesteps.astype(jnp.float32)[:, None] * freqs[None, :]
    embedding = jnp.concatenate([jnp.cos(angles), jnp.sin(angles)], 1)
    modulation = jnp.dot(embedding, time_mod.astype(jnp.float32), precision=lax.Precision.HIGHEST)
    gate = modulation[:, :WIDTH]
    scale = modulation[:, WIDTH:]
    exchange = functools.partial(lax.all_to_all, axis_name="seq", split_axis=0, concat_axis=0, tiled=True)
    gathered = exchange(jnp.concatenate([text_items, image_items], axis=2))
    groups = lax.axis_size("grp")
    staged = group_size == HEADS and groups % 2 == 0
    gathered, gate, scale = lax.optimization_barrier((gathered, gate, scale))
    if staged:
        half = lax.axis_index("grp") % 2
        rows = RowGather(frozen_out, trainee_out, half, group_size, groups)
        gathered = rows.near(gathered)
    both = attend(gathered, live, image_dev, text_dev)
    if staged:
        both = rows.far(both)
        weights, heads = rows.rows(position)
    else:
        half, heads = jnp.int32(0), jnp.arange(HEADS, dtype=jnp.int32)
        block = jnp.concatenate([frozen_out, trainee_out], axis=1)
        everything = lax.all_gather(block, "seq", axis=0, tiled=True)
        weights = [[(everything, first)] for first in (0, WIDTH // 2, WIDTH)]
    back = exchange(both).reshape(HEADS, SAMPLES, 2, image_dev, HEAD_DIM)
    cot, att = project(back, heads, half, weights, image_states, gate, scale, final_head.T)
    if group_size == HEADS:
        return reduce_by_halving(att, cot, position, group_size)
    partial = jnp.einsum("hdr,rc->hdc", att, cot, preferred_element_type=jnp.float32)
    partial = partial.reshape(HEADS * HEAD_DIM, WIDTH).astype(jnp.bfloat16)
    return lax.psum_scatter(partial, "seq", scatter_dimension=0, tiled=True).astype(jnp.float32)


def solution(mesh):
    return jax.shard_map(
        shards,
        mesh=mesh,
        in_specs=(
            P(None, "grp", None, "seq", None),
            P(None, None, "grp", None, "seq", None),
            P(None, "grp", None),
            P("grp"),
            P("grp", "seq", None),
            P("seq", None),
            P(("grp", "seq"), None),
            P(),
            P(),
        ),
        out_specs=P(("grp", "seq"), None),
        check_vma=False,
    )
```
